128 devices in a mesh: ctx: 8 (over x_hi, y), exp: 16 (over z, x_lo, core).
Axes of the slice: x: 4 (x_hi: 2, x_lo: 2; x = x_hi * 2 + x_lo), y: 4, z: 4, core: 2. Of those that a mesh axis runs over, the one named last changes fastest.
Arguments:
- queries: bfloat16 [16384, 2048], P('ctx', 'exp'), may hold values from -6 to 6
- keys: bfloat16 [16384, 2048], P('ctx', 'exp'), may hold values from -6 to 6
- values: bfloat16 [16384, 2048], P('ctx', 'exp'), may hold values from -6 to 6
- gate_input: bfloat16 [16384, 2048], P(('ctx', 'exp')), may hold values from -6 to 6
- route_ids: int32 [16384, 2], P(('ctx', 'exp')), may hold values from 0 to 31, all different within a row; in each aligned block of 128 rows (0 to 127, 128 to 255, ...) at most 16 rows name the same one
- route_gates: float32 [16384, 2], P(('ctx', 'exp')), may hold values from 0.1 to 1
- w_gate: bfloat16 [32, 2048, 512], P('exp'), may hold values from -0.125 to 0.125
- w_up: bfloat16 [32, 2048, 512], P('exp'), may hold values from -0.125 to 0.125
- w_down: bfloat16 [32, 512, 2048], P('exp'), may hold values from -0.25 to 0.25
- out_grad: bfloat16 [16384, 2048], P(('ctx', 'exp')), may hold values from -6 to 6
Outputs:
- normed: bfloat16 [16384, 2048], P(('ctx', 'exp'))
- mixed: bfloat16 [16384, 2048], P(('ctx', 'exp'))
- normed_grad: bfloat16 [16384, 2048], P(('ctx', 'exp'))
- w_gate_grad: bfloat16 [32, 2048, 512], P('exp', 'ctx')
- w_up_grad: bfloat16 [32, 2048, 512], P('exp', 'ctx')
- w_down_grad: bfloat16 [32, 512, 2048], P('exp', None, 'ctx')
The draws below stay inside these ranges and needn't reach their ends.
Inputs may be any that keep to these rules, and one draw needn't show every extreme that they name: `route_ids`: each position names two different experts. Within the 128 positions of one aligned block no expert is named by more than 16 routes, and in every draw some expert is named by exactly 16 routes of some block.
All inputs are finite; a program needn't handle non-finite values.
Results may differ from the reference program's by a relative error of at most 0.013.
Values may be sent and summed in bfloat16 or wider, within the bound.
No kernel may reach another device: no remote copies, remote signals or barrier semaphores. Data moves between devices by JAX's collectives and lax.ppermute only.
A program may use at most 128 MiB of HBM per device.

```python
import math
import jax
import jax.numpy as jnp
import numpy as np
from jax import lax

D = 2048
HEAD_DIM = 128
HIDDEN_SIZE = 512
TOK_DEV = 128
HEADS = 16
EXPERTS = 32
CAP = 16
SEQ = 16384
N_CTX = 8
N_EXP = 16


def block_scale(rng, dims, cuts, smallest, top_value):
    loudness = 1.0
    for position, parts in cuts:
        steps = jax.random.uniform(jax.random.fold_in(jax.random.fold_in(rng, 6), position), (parts,), jnp.float32, smallest / len(cuts), top_value / len(cuts))
        loudness = loudness * jnp.repeat(jnp.exp(steps), dims[position] // parts).reshape((-1,) + (1,) * (len(dims) - 1 - position))
    return loudness


def assign_block(key, own, number, rows, count, top, reach, lean):
    order = jax.random.permutation(key, count)
    heavy_load, ordinary = portions_of(count, rows * top, reach, lean, True), portions_of(count, rows * top, reach, lean, False)
    places = jnp.arange(count)

    def named(sizes, turn):
        used = int((sizes > 0).sum())
        fixed = max(1, used // 4)
        moved = fixed + (places - fixed + turn * (used - fixed)) % max(1, count - fixed)
        return jnp.zeros((count,), jnp.int32).at[order[jnp.where(places < fixed, places, moved)]].set(jnp.asarray(sizes, jnp.int32))

    sizes = jnp.where(number % 4 == 0, named(heavy_load, number // 4), named(ordinary, number - number // 4 - 1))
    mixed = jax.random.permutation(jax.random.fold_in(own, 3), count)
    giver, taker = mixed[0:count // 2 * 2:2], mixed[1:count // 2 * 2:2]
    margin = jnp.minimum(sizes[giver] - 1, reach - sizes[taker]) // 2
    margin = jnp.where((giver == order[0]) | (taker == order[0]) | (sizes[taker] == 0), 0, jnp.maximum(margin, 0))
    moved = jax.random.randint(jax.random.fold_in(own, 4), (count // 2,), 0, 1 << 20) % (margin + 1)
    sizes = sizes.at[giver].add(-moved).at[taker].add(moved)
    items = jnp.searchsorted(jnp.cumsum(sizes), jnp.arange(rows * top), side="right").astype(jnp.int32)
    table = items.reshape(top, rows).T
    table = table[jax.random.permutation(jax.random.fold_in(own, 1), rows)]
    turn = jax.random.randint(jax.random.fold_in(own, 2), (rows, 1), 0, top)
    return jnp.take_along_axis(table, (jnp.arange(top)[None, :] + turn) % top, axis=1)


def portions_of(number_of, total, most, slope, full):
    portions = [(1 << 20) // math.isqrt(standing ** slope) + 1 for standing in range(1, number_of + 1)]
    largest = most if full else min(most, max(-(-total // number_of), total * portions[0] // sum(portions)))
    least = 1 if total - largest >= number_of - 1 else 0
    holding, surplus = [largest] + [least] * (number_of - 1), total - largest - least * (number_of - 1)
    while surplus > 0:
        movable = [i for i in range(1, number_of) if holding[i] < largest] or [i for i in range(1, number_of) if holding[i] < most]
        pool, left = sum([portions[i] for i in movable]), surplus
        for i in movable:
            extra = min(most - holding[i], max(1, left * portions[i] // pool), surplus)
            holding[i] = holding[i] + extra
            surplus = surplus - extra
    return np.array(holding)


def scatter_about(rng, shape, scale, most, pieces=(), kind=jnp.bfloat16):
    array = jax.random.normal(rng, shape, jnp.float32) * scale
    if len(pieces) > 0:
        array = block_scale(rng, shape, pieces, -0.22, 0.18) * array
    return jnp.clip(array, min=-most, max=most).astype(kind)


def setup_inputs(seed: int = 0) -> dict:
    splits = jax.random.split(jax.random.key(seed), 11)
    queries = scatter_about(splits[0], (SEQ, D), 1.0, 6.0, ((0, 8), (1, 16)))
    keys = scatter_about(splits[1], (SEQ, D), 1.0, 6.0, ((0, 8), (1, 16)))
    values = scatter_about(splits[2], (SEQ, D), 1.0, 6.0, ((0, 8), (1, 16)))
    gate_input = scatter_about(splits[3], (SEQ, D), 1.0, 6.0, ((0, 128),))
    route_ids_keys = jax.random.split(jax.random.fold_in(splits[4], 1), SEQ // TOK_DEV)
    route_ids_turns = jax.random.permutation(jax.random.fold_in(splits[4], 3), SEQ // TOK_DEV)
    route_ids = jax.vmap(lambda own, number: assign_block(jax.random.fold_in(splits[4], 2), own, number, TOK_DEV, EXPERTS, 2, CAP, 2))(route_ids_keys, route_ids_turns).reshape((SEQ, 2))
    route_gates = jnp.clip(0.1 + 0.9 * jax.random.uniform(splits[5], (SEQ, 2), jnp.float32) ** block_scale(splits[5], (SEQ, 2), ((0, 128),), -0.2, 0.2), 0.1, 1.0)
    w_gate = scatter_about(splits[6], (EXPERTS, D, HIDDEN_SIZE), D ** -0.5, 0.125, ((0, 16),))
    w_up = scatter_about(splits[7], (EXPERTS, D, HIDDEN_SIZE), D ** -0.5, 0.125, ((0, 16),))
    w_down = scatter_about(splits[8], (EXPERTS, HIDDEN_SIZE, D), HIDDEN_SIZE ** -0.5, 0.25, ((0, 16),))
    out_grad = scatter_about(splits[9], (SEQ, D), 1.0, 6.0, ((0, 128),))
    return dict(queries=queries, keys=keys, values=values, gate_input=gate_input, route_ids=route_ids, route_gates=route_gates, w_gate=w_gate, w_up=w_up, w_down=w_down, out_grad=out_grad)


def silu_grad(value):
    sigma = jax.nn.sigmoid(value)
    return sigma * (1.0 + value * (1.0 - sigma))

def attention(queries, keys, values):
    block_rows = TOK_DEV * N_EXP
    block_count = SEQ // block_rows
    query_heads = queries.reshape(block_count, block_rows, HEADS, HEAD_DIM)
    key_heads = keys.reshape(block_count, block_rows, HEADS, HEAD_DIM)
    value_heads = values.reshape(block_count, block_rows, HEADS, HEAD_DIM)
    scale = 1.0 / math.sqrt(HEAD_DIM)
    positions = jnp.arange(block_rows, dtype=jnp.int32)

    def one_query(query_index):
        query_block = lax.dynamic_index_in_dim(query_heads, query_index, 0, keepdims=False).astype(jnp.float32)

        def over_keys(running, key_index):

            def compute(inner):
                key_block = lax.dynamic_index_in_dim(key_heads, key_index, 0, keepdims=False).astype(jnp.float32)
                value_block = lax.dynamic_index_in_dim(value_heads, key_index, 0, keepdims=False).astype(jnp.float32)
                scores = jnp.einsum('qhd,khd->hqk', query_block, key_block) * scale
                allowed = (query_index * block_rows + positions)[:, None] >= (key_index * block_rows + positions)[None, :]
                weight = jnp.where(allowed[None], jax.nn.silu(scores), 0.0).astype(jnp.bfloat16)
                weight = lax.optimization_barrier(weight).astype(jnp.float32)
                return inner + jnp.einsum('hqk,khd->qhd', weight, value_block)
            return (lax.cond(key_index <= query_index, compute, lambda inner: inner, running), None)
        initial = jnp.zeros((block_rows, HEADS, HEAD_DIM), jnp.float32)
        result, unused = lax.scan(over_keys, initial, jnp.arange(block_count, dtype=jnp.int32))
        return result
    blocks = lax.map(one_query, jnp.arange(block_count, dtype=jnp.int32))
    return blocks.reshape(SEQ, HEADS * HEAD_DIM).astype(jnp.bfloat16)

def group_sum(left, right):
    group_rows = N_EXP * CAP
    left_groups = left.reshape(N_CTX, group_rows, left.shape[1]).astype(jnp.float32)
    right_groups = right.reshape(N_CTX, group_rows, right.shape[1]).astype(jnp.float32)
    partial_terms = jnp.einsum('crd,crh->cdh', left_groups, right_groups).astype(jnp.bfloat16)
    partial_terms = lax.optimization_barrier(partial_terms).astype(jnp.float32)
    return lax.optimization_barrier(jnp.sum(partial_terms, axis=0)).astype(jnp.bfloat16)

def reference(queries, keys, values, gate_input, route_ids, route_gates, w_gate, w_up, w_down, out_grad):
    attended = attention(queries, keys, values).astype(jnp.float32)
    mean_rows = lax.optimization_barrier(jnp.mean(attended, axis=1, keepdims=True))
    centred = attended - mean_rows
    variance = lax.optimization_barrier(jnp.mean(centred * centred, axis=1, keepdims=True))
    normed = (centred * lax.rsqrt(variance + 1e-05) * gate_input.astype(jnp.float32)).astype(jnp.bfloat16)
    block_count = SEQ // TOK_DEV
    flat_ids = route_ids.reshape(block_count, TOK_DEV * 2)
    onehot = (flat_ids[:, :, None] == jnp.arange(EXPERTS, dtype=jnp.int32)[None, None, :]).astype(jnp.int32)
    slot_ids = lax.optimization_barrier(jnp.sum((jnp.cumsum(onehot, axis=1) - onehot) * onehot, axis=2))
    row_ids = (jnp.arange(block_count, dtype=jnp.int32)[:, None] * CAP + slot_ids).reshape(-1).astype(jnp.int32)
    expert_ids = flat_ids.reshape(-1).astype(jnp.int32)
    buffer_rows = block_count * CAP

    def scatter_rows(source_rows):
        return jnp.zeros((EXPERTS, buffer_rows, D), jnp.bfloat16).at[expert_ids, row_ids].set(source_rows)
    expert_inputs = scatter_rows(jnp.repeat(normed, 2, axis=0))
    scaled_grad = (route_gates[:, :, None] * out_grad.astype(jnp.float32)[:, None, :]).astype(jnp.bfloat16)
    expert_grads = scatter_rows(scaled_grad.reshape(SEQ * 2, D))

    def one_expert(items):
        inputs, grads, gate_weight, up_weight, down_weight = items
        gate_pre = jnp.dot(inputs, gate_weight, preferred_element_type=jnp.float32)
        up_pre = jnp.dot(inputs, up_weight, preferred_element_type=jnp.float32)
        hidden = (jax.nn.silu(gate_pre) * up_pre).astype(jnp.bfloat16)
        output = jnp.dot(hidden, down_weight, preferred_element_type=jnp.float32).astype(jnp.bfloat16)
        hidden_grad = jnp.dot(grads, down_weight.T, preferred_element_type=jnp.float32)
        gate_grad = (hidden_grad * up_pre * silu_grad(gate_pre)).astype(jnp.bfloat16)
        up_grad = (hidden_grad * jax.nn.silu(gate_pre)).astype(jnp.bfloat16)
        input_grad = (jnp.dot(gate_grad, gate_weight.T, preferred_element_type=jnp.float32) + jnp.dot(up_grad, up_weight.T, preferred_element_type=jnp.float32)).astype(jnp.bfloat16)
        gate_wgrad = group_sum(inputs, gate_grad)
        up_wgrad = group_sum(inputs, up_grad)
        down_wgrad = group_sum(hidden, grads)
        return (output, input_grad, gate_wgrad, up_wgrad, down_wgrad)
    outputs, input_grads, gate_wgrads, up_wgrads, down_wgrads = lax.map(one_expert, (expert_inputs, expert_grads, w_gate, w_up, w_down))
    picked = outputs[expert_ids, row_ids].reshape(SEQ, 2, D).astype(jnp.float32)
    mixed = lax.optimization_barrier(jnp.sum(picked * route_gates[:, :, None], axis=1)).astype(jnp.bfloat16)
    picked_grads = input_grads[expert_ids, row_ids].reshape(SEQ, 2, D).astype(jnp.float32)
    normed_grad = lax.optimization_barrier(jnp.sum(picked_grads, axis=1)).astype(jnp.bfloat16)
    return (normed, mixed, normed_grad, gate_wgrads, up_wgrads, down_wgrads)
```

```python
import math

import jax
import jax.numpy as jnp
from jax import lax
from jax.experimental import pallas as pl
from jax.experimental.pallas import tpu as pltpu
from jax.sharding import PartitionSpec as P

HEAD_DIM = 128
EXPERTS = 32
CAP = 16
N_EXP = 16
TOK = 128
ROWS = N_EXP * CAP
TQ = 256
TK = 512
F32 = jnp.float32
BF16 = jnp.bfloat16


def vmem():
    return pl.BlockSpec(memory_space=pltpu.VMEM)


def smem():
    return pl.BlockSpec(memory_space=pltpu.SMEM)


def mm(a, b, ca, cb):
    return lax.dot_general(a, b, (((ca,), (cb,)), ((), ())), preferred_element_type=F32)


def half_silu(scores):
    h = scores * (0.5 / math.sqrt(HEAD_DIM))
    return h + h * jnp.tanh(h)


def make_attend(kinds, first, last, rows):
    count = len(kinds)

    def kernel(*refs):
        flags, q_ref = refs[0], refs[1]
        kv_refs = refs[2 : 2 + count]
        acc_in = None if first else refs[2 + count]
        out_ref = refs[-2] if last else refs[-1]
        acc = refs[-1]

        if first:
            acc[...] = jnp.zeros_like(acc)
        elif last:
            acc[...] = acc_in[...]
        for n, kv in enumerate(kv_refs):
            if kinds[n]:

                def q_step(i, carry, kv=kv):
                    rows_i = pl.ds(pl.multiple_of(i * TQ, TQ), TQ)
                    q = q_ref[rows_i, :]

                    def k_step(j, part):
                        rows_j = pl.ds(pl.multiple_of(j * TQ, TQ), TQ)
                        w = half_silu(mm(q, kv[0, rows_j, :], 1, 1)).astype(BF16)
                        return part + mm(w, kv[1, rows_j, :], 1, 0)

                    part = lax.fori_loop(0, i, k_step, jnp.zeros((TQ, HEAD_DIM), F32))
                    s = half_silu(mm(q, kv[0, rows_i, :], 1, 1))
                    allowed = lax.broadcasted_iota(jnp.int32, (TQ, TQ), 0) >= lax.broadcasted_iota(
                        jnp.int32, (TQ, TQ), 1
                    )
                    w = jnp.where(allowed, s, 0.0).astype(BF16)
                    acc[rows_i, :] += part + mm(w, kv[1, rows_i, :], 1, 0)
                    return carry

                lax.fori_loop(0, rows // TQ, q_step, 0)
            else:

                @pl.when(flags[n] != 0)
                def _(kv=kv):
                    def q_step(i, carry):
                        rows_i = pl.ds(pl.multiple_of(i * TQ, TQ), TQ)
                        q = q_ref[rows_i, :]
                        part = acc[rows_i, :]
                        for j in range(rows // TK):
                            rows_j = pl.ds(j * TK, TK)
                            w = half_silu(mm(q, kv[0, rows_j, :], 1, 1)).astype(BF16)
                            part = part + mm(w, kv[1, rows_j, :], 1, 0)
                        acc[rows_i, :] = part
                        return carry

                    lax.fori_loop(0, rows // TQ, q_step, 0)

        if last:
            out_ref[...] = acc[...].astype(BF16)

    def call(flags, q, kvs, acc):
        args = [flags, q, *kvs] + ([] if first else [acc])
        specs = [smem()] + [vmem()] * (len(args) - 1)
        return pl.pallas_call(
            kernel,
            out_shape=jax.ShapeDtypeStruct((rows, HEAD_DIM), BF16 if last else F32),
            in_specs=specs,
            out_specs=vmem(),
            scratch_shapes=[pltpu.VMEM((rows, HEAD_DIM), F32)] if last else [],
            input_output_aliases={} if (first or last) else {len(args) - 1: 0},
            name="attend_last" if last else "attend",
        )(*args)

    return call


def attend_alias(kinds, rows):
    count = len(kinds)

    def kernel(*refs):
        flags, q_ref = refs[0], refs[1]
        kv_refs = refs[2 : 2 + count]
        acc_in, acc = refs[2 + count], refs[3 + count]
        acc[...] = acc_in[...]
        for n, kv in enumerate(kv_refs):

            @pl.when(flags[n] != 0)
            def _(kv=kv):
                def q_step(i, carry):
                    rows_i = pl.ds(pl.multiple_of(i * TQ, TQ), TQ)
                    q = q_ref[rows_i, :]
                    part = acc[rows_i, :]
                    for j in range(rows // TK):
                        rows_j = pl.ds(j * TK, TK)
                        w = half_silu(mm(q, kv[0, rows_j, :], 1, 1)).astype(BF16)
                        part = part + mm(w, kv[1, rows_j, :], 1, 0)
                    acc[rows_i, :] = part
                    return carry

                lax.fori_loop(0, rows // TQ, q_step, 0)

    def call(flags, q, kvs, acc):
        return pl.pallas_call(
            kernel,
            out_shape=jax.ShapeDtypeStruct((rows, HEAD_DIM), F32),
            in_specs=[smem()] + [vmem()] * (count + 2),
            out_specs=vmem(),
            name="attend_mid",
        )(flags, q, *kvs, acc)

    return call


def route_kernel(ids_ref, gates_ref, grad_ref, pick0_ref, pick1_ref, send_ref):
    ids = ids_ref[...]
    expert = lax.broadcasted_iota(jnp.int32, (EXPERTS, TOK), 0)
    one0 = (expert == ids[0:1, :]).astype(F32)
    one1 = (expert == ids[1:2, :]).astype(F32)
    earlier = lax.broadcasted_iota(jnp.int32, (TOK, TOK), 0) < lax.broadcasted_iota(
        jnp.int32, (TOK, TOK), 1
    )
    counts = mm((one0 + one1).astype(BF16), earlier.astype(F32).astype(BF16), 1, 0)
    slot0 = jnp.sum(one0 * counts, axis=0, keepdims=True).astype(jnp.int32)
    slot1 = jnp.sum(one1 * (counts + one0), axis=0, keepdims=True).astype(jnp.int32)
    row = lax.broadcasted_iota(jnp.int32, (EXPERTS * CAP, TOK), 0)
    pick0 = (row == ids[0:1, :] * CAP + slot0).astype(F32).astype(BF16)
    pick1 = (row == ids[1:2, :] * CAP + slot1).astype(F32).astype(BF16)
    pick0_ref[...] = pick0
    pick1_ref[...] = pick1
    grad = grad_ref[...].astype(F32)
    scaled0 = (gates_ref[:, 0:1] * grad).astype(BF16)
    scaled1 = (gates_ref[:, 1:2] * grad).astype(BF16)
    sent = mm(pick0, scaled0, 1, 0) + mm(pick1, scaled1, 1, 0)
    send_ref[...] = sent.astype(BF16).reshape(send_ref.shape)


def norm_kernel(tok_ref, gate_ref, pick0_ref, pick1_ref, normed_ref, send_ref):
    heads = [tok_ref[h].astype(F32) for h in range(tok_ref.shape[0])]
    width = HEAD_DIM * len(heads)
    total = heads[0]
    for h in heads[1:]:
        total = total + h
    mean = jnp.sum(total, axis=1, keepdims=True) * (1.0 / width)
    squares = None
    for h in heads:
        c = h - mean
        squares = c * c if squares is None else squares + c * c
    variance = jnp.sum(squares, axis=1, keepdims=True) * (1.0 / width)
    scale = lax.rsqrt(variance + 1e-05)
    for n, h in enumerate(heads):
        cols = slice(n * HEAD_DIM, (n + 1) * HEAD_DIM)
        normed_ref[:, cols] = ((h - mean) * scale * gate_ref[:, cols].astype(F32)).astype(BF16)
    pick = pick0_ref[...] + pick1_ref[...]
    send_ref[...] = mm(pick, normed_ref[...], 1, 0).astype(BF16).reshape(send_ref.shape)


def hidden_grad_kernel(grad_ref, down_ref, out_ref):
    grads = grad_ref[...].reshape(ROWS, grad_ref.shape[2])
    out_ref[0] = mm(grads, down_ref[0], 1, 1)


def expert_in_kernel(in_ref, hg_ref, gate_ref, up_ref, hidden_ref, gg_ref, ug_ref):
    rows = in_ref[...].reshape(ROWS, in_ref.shape[2])
    gate_pre = mm(rows, gate_ref[0], 1, 0)
    up_pre = mm(rows, up_ref[0], 1, 0)
    sigma = jax.nn.sigmoid(gate_pre)
    silu = gate_pre * sigma
    hidden_grad = hg_ref[0]
    hidden_ref[0] = (silu * up_pre).astype(BF16)
    gg_ref[0] = (hidden_grad * up_pre * (sigma * (1.0 + gate_pre * (1.0 - sigma)))).astype(BF16)
    ug_ref[0] = (hidden_grad * silu).astype(BF16)


def up_grad_kernel(idx_ref, in_ref, ug_ref, keep_ref, send_ref):
    step = pl.program_id(0)

    def part(e):
        rows = in_ref[:, e * CAP : (e + 1) * CAP, :].reshape(ROWS, in_ref.shape[2])
        return mm(rows, ug_ref[e], 0, 0).astype(BF16)

    @pl.when(step < 4)
    def _():
        for e in range(2):
            send_ref[0, e] = part(e)

    @pl.when(step >= 4)
    def _():
        for e in range(2):
            keep_ref[0, e] = part(e)


def gate_down_kernel(idx_ref, in_ref, grad_ref, gg_ref, hidden_ref, y1_ref, y2_ref, y3_ref, y0_ref):
    step = pl.program_id(0)
    outs = (y1_ref, y2_ref, y3_ref, y0_ref)
    for n, out in enumerate(outs):

        @pl.when(step // 2 == n)
        def _(out=out):
            for e in range(2):
                rows = in_ref[:, e * CAP : (e + 1) * CAP, :].reshape(ROWS, in_ref.shape[2])
                grads = grad_ref[:, e * CAP : (e + 1) * CAP, :].reshape(ROWS, in_ref.shape[2])
                out[0, 0, e] = mm(rows, gg_ref[e], 0, 0).astype(BF16)
                out[0, 1, e] = mm(grads, hidden_ref[e], 0, 0).astype(BF16)


def expert_out_kernel(hidden_ref, down_ref, out_ref):
    out_ref[...] = mm(hidden_ref[0], down_ref[0], 1, 0).astype(BF16).reshape(out_ref.shape)


def input_grad_kernel(gg_ref, ug_ref, gate_ref, up_ref, out_ref):
    total = mm(gg_ref[0], gate_ref[0], 1, 1) + mm(ug_ref[0], up_ref[0], 1, 1)
    out_ref[...] = total.astype(BF16).reshape(out_ref.shape)


def mixed_kernel(back_ref, pick0_ref, pick1_ref, gates_ref, out_ref):
    back = back_ref[...].reshape(EXPERTS * CAP, back_ref.shape[2])
    first = mm(pick0_ref[...], back, 0, 0) * gates_ref[:, 0:1]
    second = mm(pick1_ref[...], back, 0, 0) * gates_ref[:, 1:2]
    out_ref[...] = (first + second).astype(BF16)


def normed_grad_kernel(back_ref, pick0_ref, pick1_ref, out_ref):
    back = back_ref[...].reshape(EXPERTS * CAP, back_ref.shape[2])
    pick = pick0_ref[...] + pick1_ref[...]
    out_ref[...] = mm(pick, back, 0, 0).astype(BF16)


def move_y(value, distance, keep=lambda hi, y: True):
    pairs = [
        (hi * 4 + y, hi * 4 + (y + distance) % 4)
        for hi in range(2)
        for y in range(4)
        if keep(hi, y)
    ]
    return lax.ppermute(value, "ctx", pairs)


def move_x(value, both=True):
    pairs = [(y, 4 + y) for y in range(4)]
    if both:
        pairs += [(4 + y, y) for y in range(4)]
    return lax.ppermute(value, "ctx", pairs)


def exchange(value):
    return lax.all_to_all(value, "exp", split_axis=0, concat_axis=0, tiled=True)


def body(queries, keys, values, gate_input, route_ids, route_gates, w_gate, w_up, w_down, out_grad):
    rows = queries.shape[0]
    width = gate_input.shape[1]
    hid = w_gate.shape[2]
    ctx = lax.axis_index("ctx")
    hi, y = ctx // 4, ctx % 4
    full = jax.ShapeDtypeStruct

    kv = jnp.stack([keys, values])
    from_x = move_x(kv, both=False)
    from_y1 = move_y(kv, 1, lambda hi, y: y < 3)
    from_y2 = move_y(kv, 2, lambda hi, y: hi == 0 or y < 2)
    from_y3 = move_y(kv, 3, lambda hi, y: y == 0)
    low = lambda h, y: h == 1
    from_xy1 = move_y(from_x, 1, low)
    from_xy3 = move_y(from_x, 3, low)
    from_xy2 = move_x(from_y2, both=False)

    pick0, pick1, send_grads = pl.pallas_call(
        route_kernel,
        out_shape=(
            full((EXPERTS * CAP, TOK), BF16),
            full((EXPERTS * CAP, TOK), BF16),
            full((N_EXP, 2 * CAP, width), BF16),
        ),
        in_specs=[vmem()] * 3,
        out_specs=(vmem(),) * 3,
        name="route",
    )(route_ids.T, route_gates, out_grad)
    recv_grads = exchange(send_grads)

    flag = lambda *conds: jnp.stack([c.astype(jnp.int32) for c in conds])
    high = hi == 1
    acc = make_attend((True,), True, False, rows)(flag(high), queries, [kv], None)
    acc = attend_alias((False, False), rows)(flag(y >= 1, high), queries, [from_y1, from_x], acc)
    acc = attend_alias((False, False), rows)(
        flag(y >= 2, y >= 3), queries, [from_y2, from_y3], acc
    )
    attended = make_attend((False, False, False), False, True, rows)(
        flag(high, high, high), queries, [from_xy1, from_xy3, from_xy2], acc
    )

    expert_block = pl.BlockSpec((N_EXP, CAP, width), lambda e: (0, e, 0))
    in_weight = pl.BlockSpec((1, width, hid), lambda e: (e, 0, 0))
    out_weight = pl.BlockSpec((1, hid, width), lambda e: (e, 0, 0))
    act_block = pl.BlockSpec((1, ROWS, hid), lambda e: (e, 0, 0))
    hidden_grad = pl.pallas_call(
        hidden_grad_kernel,
        grid=(2,),
        out_shape=full((2, ROWS, hid), F32),
        in_specs=[expert_block, out_weight],
        out_specs=act_block,
        name="hidden_grad",
    )(recv_grads, w_down)

    token_heads = exchange(attended.reshape(N_EXP, TOK, HEAD_DIM))
    normed, send_inputs = pl.pallas_call(
        norm_kernel,
        out_shape=(full((TOK, width), BF16), full((N_EXP, 2 * CAP, width), BF16)),
        in_specs=[vmem()] * 4,
        out_specs=(vmem(),) * 2,
        name="norm",
    )(token_heads, gate_input, pick0, pick1)
    recv_inputs = exchange(send_inputs)

    act = full((2, ROWS, hid), BF16)
    hidden, gate_grad, up_grad = pl.pallas_call(
        expert_in_kernel,
        grid=(2,),
        out_shape=(act, act, act),
        in_specs=[expert_block, act_block, in_weight, in_weight],
        out_specs=(act_block,) * 3,
        name="expert_in",
    )(recv_inputs, hidden_grad, w_gate, w_up)

    cols = width // 8
    turn = jnp.arange(4, dtype=jnp.int32)
    x_order = jnp.concatenate([(1 - hi) * 4 + (y + turn) % 4, hi * 4 + (y + turn) % 4])
    far = (turn + 1) % 4
    y_order = jnp.stack(
        [hi * 4 + (y + far) % 4, (1 - hi) * 4 + (y + far) % 4], axis=1
    ).reshape(8)
    slice_spec = pl.BlockSpec((N_EXP, 2 * CAP, cols), lambda s, idx: (0, 0, idx[s]))
    act_all = pl.BlockSpec((2, ROWS, hid), lambda s, idx: (0, 0, 0))
    half = full((4, 2, cols, hid), BF16)
    up_keep, up_send = pl.pallas_call(
        up_grad_kernel,
        grid_spec=pltpu.PrefetchScalarGridSpec(
            num_scalar_prefetch=1,
            grid=(8,),
            in_specs=[slice_spec, act_all],
            out_specs=(
                pl.BlockSpec((1, 2, cols, hid), lambda s, idx: (jnp.maximum(s - 4, 0), 0, 0, 0)),
                pl.BlockSpec((1, 2, cols, hid), lambda s, idx: (jnp.minimum(s, 3), 0, 0, 0)),
            ),
        ),
        out_shape=(half, half),
        name="up_wgrad",
    )(x_order, recv_inputs, up_grad)
    up_got = move_x(up_send)

    def y_spec(n):
        return pl.BlockSpec(
            (1, 2, 2, cols, hid), lambda s, idx: (jnp.clip(s - 2 * n, 0, 1), 0, 0, 0, 0)
        )

    quarter = full((2, 2, 2, cols, hid), BF16)
    y1, y2, y3, y0 = pl.pallas_call(
        gate_down_kernel,
        grid_spec=pltpu.PrefetchScalarGridSpec(
            num_scalar_prefetch=1,
            grid=(8,),
            in_specs=[slice_spec, slice_spec, act_all, act_all],
            out_specs=tuple(y_spec(n) for n in range(4)),
        ),
        out_shape=(quarter,) * 4,
        name="gate_down_wgrad",
    )(y_order, recv_inputs, recv_grads, gate_grad, hidden)
    g1, g2, g3 = move_y(y1, 1), move_y(y2, 2), move_y(y3, 3)

    routed = full((N_EXP, 2 * CAP, width), BF16)
    expert_out = pl.pallas_call(
        expert_out_kernel,
        grid=(2,),
        out_shape=routed,
        in_specs=[act_block, out_weight],
        out_specs=expert_block,
        name="expert_out",
    )(hidden, w_down)
    back_out = exchange(expert_out)
    input_grad = pl.pallas_call(
        input_grad_kernel,
        grid=(2,),
        out_shape=routed,
        in_specs=[act_block, act_block, in_weight, in_weight],
        out_specs=expert_block,
        name="input_grad",
    )(gate_grad, up_grad, w_gate, w_up)
    back_grad = exchange(input_grad)

    token = full((TOK, width), BF16)
    mixed = pl.pallas_call(
        mixed_kernel, out_shape=token, in_specs=[vmem()] * 4, out_specs=vmem(), name="mixed"
    )(back_out, pick0, pick1, route_gates)
    normed_grad = pl.pallas_call(
        normed_grad_kernel, out_shape=token, in_specs=[vmem()] * 3, out_specs=vmem(), name="ngrad"
    )(back_grad, pick0, pick1)

    wide = lambda v: v.astype(F32)
    up_part = wide(up_keep) + wide(up_got)
    up_sums = [up_part[n].astype(BF16) for n in range(4)]
    u1, u2, u3 = (move_y(up_sums[n], n) for n in (1, 2, 3))
    gd_send = (wide(y0[1]) + wide(g1[1]) + wide(g2[1]) + wide(g3[1])).astype(BF16)
    gd_got = move_x(gd_send)
    gd = wide(y0[0]) + wide(g1[0]) + wide(g2[0]) + wide(g3[0]) + wide(gd_got)
    gate_sum = gd[0].astype(BF16)
    down_sum = jnp.swapaxes(gd[1], 1, 2).astype(BF16)
    up_sum = (up_part[0] + wide(u1) + wide(u2) + wide(u3)).astype(BF16)
    return (normed, mixed, normed_grad, gate_sum, up_sum, down_sum)


def solution(mesh):
    in_specs = (
        P("ctx", "exp"),
        P("ctx", "exp"),
        P("ctx", "exp"),
        P(("ctx", "exp"), None),
        P(("ctx", "exp"), None),
        P(("ctx", "exp"), None),
        P("exp", None, None),
        P("exp", None, None),
        P("exp", None, None),
        P(("ctx", "exp"), None),
    )
    out_specs = (
        P(("ctx", "exp"), None),
        P(("ctx", "exp"), None),
        P(("ctx", "exp"), None),
        P("exp", "ctx", None),
        P("exp", "ctx", None),
        P("exp", None, "ctx"),
    )
    return jax.shard_map(body, mesh=mesh, in_specs=in_specs, out_specs=out_specs, check_vma=False)
```

```python
import math

import jax
import jax.numpy as jnp
from jax import lax
from jax.experimental import pallas as pl
from jax.experimental.pallas import tpu as pltpu
from jax.sharding import PartitionSpec as P


HEAD_DIM = 128
EXPERTS = 32
CAP = 16
N_EXP = 16
TOK = 128
ROWS = N_EXP * CAP
TQ = 512
TK = 256
F32 = jnp.float32
BF16 = jnp.bfloat16


def vmem():
    return pl.BlockSpec(memory_space=pltpu.VMEM)


def smem():
    return pl.BlockSpec(memory_space=pltpu.SMEM)


def mm(a, b, ca, cb):
    return lax.dot_general(a, b, (((ca,), (cb,)), ((), ())), preferred_element_type=F32)


def half_silu(scores):
    h = scores * (0.5 / math.sqrt(HEAD_DIM))
    return h + h * jnp.tanh(h)


def attend_tile(q, key_t, value, masked_from):
    w = half_silu(mm(q, key_t, 1, 0))
    if masked_from is not None:
        row = lax.broadcasted_iota(jnp.int32, w.shape, 0)
        col = lax.broadcasted_iota(jnp.int32, w.shape, 1)
        w = jnp.where(row >= col + masked_from, w, 0.0)
    return mm(w.astype(BF16), value, 1, 0)


def add_block(q_ref, turned, value, acc, rows):
    def q_step(i, carry):
        rows_i = pl.ds(pl.multiple_of(i * TQ, TQ), TQ)
        q = q_ref[rows_i, :]
        part = acc[rows_i, :]
        for j in range(rows // TK):
            rows_j = pl.ds(j * TK, TK)
            part = part + attend_tile(q, turned[:, rows_j], value[rows_j, :], None)
        acc[rows_i, :] = part
        return carry

    lax.fori_loop(0, rows // TQ, q_step, 0)


def attend_own(q, kv):
    rows = q.shape[0]

    def kernel(q_ref, kv, acc, turned):
        turned[...] = kv[0].T
        for i in range(rows // TQ):
            rows_i = pl.ds(i * TQ, TQ)
            part = jnp.zeros((TQ, HEAD_DIM), F32)
            for j in range((i + 1) * TQ // TK):
                rows_j = pl.ds(j * TK, TK)
                gap = j * TK - i * TQ
                part = part + attend_tile(
                    q_ref[rows_i, :], turned[:, rows_j], kv[1, rows_j, :], gap if gap >= 0 else None
                )
            acc[rows_i, :] = part

    return pl.pallas_call(
        kernel,
        out_shape=jax.ShapeDtypeStruct((rows, HEAD_DIM), F32),
        in_specs=[vmem()] * 2,
        out_specs=vmem(),
        scratch_shapes=[pltpu.VMEM((HEAD_DIM, rows), BF16)],
        name="attend_own",
    )(q, kv)


def attend(flags, q, kvs, base, extra, out_type):
    rows = q.shape[0]
    count = len(kvs)
    given = [v for v in (base, extra) if v is not None]

    def kernel(*refs):
        flags_ref, q_ref = refs[0], refs[1]
        kv_refs = refs[2 : 2 + count]
        base_ref = refs[2 + count] if base is not None else None
        extra_ref = refs[1 + count + len(given)] if extra is not None else None
        out, acc, turned, value = refs[-4:]
        acc[...] = jnp.zeros_like(acc) if base is None else base_ref[...]

        def one(n, carry):
            @pl.when(flags_ref[n] != 0)
            def _():
                for m, kv in enumerate(kv_refs):

                    @pl.when(n == m)
                    def _(kv=kv):
                        turned[...] = kv[0].T
                        value[...] = kv[1]

                add_block(q_ref, turned, value, acc, rows)

            return carry

        lax.fori_loop(0, count, one, 0)
        total = acc[...]
        if extra is not None:
            total = total + extra_ref[...].astype(F32)
        out[...] = total.astype(out_type)

    return pl.pallas_call(
        kernel,
        out_shape=jax.ShapeDtypeStruct((rows, HEAD_DIM), out_type),
        in_specs=[smem()] + [vmem()] * (1 + count + len(given)),
        out_specs=vmem(),
        scratch_shapes=[
            pltpu.VMEM((rows, HEAD_DIM), F32),
            pltpu.VMEM((HEAD_DIM, rows), BF16),
            pltpu.VMEM((rows, HEAD_DIM), BF16),
        ],
    )(flags, q, *kvs, *given)


def route_kernel(ids_ref, gates_ref, grad_ref, pick0_ref, pick1_ref, send_ref):
    ids = ids_ref[...]
    expert = lax.broadcasted_iota(jnp.int32, (EXPERTS, TOK), 0)
    one0 = (expert == ids[0:1, :]).astype(F32)
    one1 = (expert == ids[1:2, :]).astype(F32)
    earlier = lax.broadcasted_iota(jnp.int32, (TOK, TOK), 0) < lax.broadcasted_iota(
        jnp.int32, (TOK, TOK), 1
    )
    counts = mm((one0 + one1).astype(BF16), earlier.astype(F32).astype(BF16), 1, 0)
    slot0 = jnp.sum(one0 * counts, axis=0, keepdims=True).astype(jnp.int32)
    slot1 = jnp.sum(one1 * (counts + one0), axis=0, keepdims=True).astype(jnp.int32)
    row = lax.broadcasted_iota(jnp.int32, (EXPERTS * CAP, TOK), 0)
    pick0 = (row == ids[0:1, :] * CAP + slot0).astype(F32).astype(BF16)
    pick1 = (row == ids[1:2, :] * CAP + slot1).astype(F32).astype(BF16)
    pick0_ref[...] = pick0
    pick1_ref[...] = pick1
    grad = grad_ref[...].astype(F32)
    scaled0 = (gates_ref[:, 0:1] * grad).astype(BF16)
    scaled1 = (gates_ref[:, 1:2] * grad).astype(BF16)
    sent = mm(pick0, scaled0, 1, 0) + mm(pick1, scaled1, 1, 0)
    send_ref[...] = sent.astype(BF16).reshape(send_ref.shape)


def norm_kernel(tok_ref, gate_ref, pick0_ref, pick1_ref, normed_ref, send_ref):
    heads = [tok_ref[h].astype(F32) for h in range(tok_ref.shape[0])]
    width = HEAD_DIM * len(heads)
    total = heads[0]
    for h in heads[1:]:
        total = total + h
    mean = jnp.sum(total, axis=1, keepdims=True) * (1.0 / width)
    squares = None
    for h in heads:
        c = h - mean
        squares = c * c if squares is None else squares + c * c
    variance = jnp.sum(squares, axis=1, keepdims=True) * (1.0 / width)
    scale = lax.rsqrt(variance + 1e-05)
    for n, h in enumerate(heads):
        cols = slice(n * HEAD_DIM, (n + 1) * HEAD_DIM)
        normed_ref[:, cols] = ((h - mean) * scale * gate_ref[:, cols].astype(F32)).astype(BF16)
    pick = pick0_ref[...] + pick1_ref[...]
    send_ref[...] = mm(pick, normed_ref[...], 1, 0).astype(BF16).reshape(send_ref.shape)


def hidden_grad_kernel(grad_ref, down_ref, out_ref):
    grads = grad_ref[...].reshape(ROWS, grad_ref.shape[2])
    out_ref[0] = mm(grads, down_ref[0], 1, 1)


def expert_in_kernel(in_ref, hg_ref, gate_ref, up_ref, hidden_ref, gg_ref, ug_ref):
    rows = in_ref[...].reshape(ROWS, in_ref.shape[2])
    gate_pre = mm(rows, gate_ref[0], 1, 0)
    up_pre = mm(rows, up_ref[0], 1, 0)
    sigma = jax.nn.sigmoid(gate_pre)
    silu = gate_pre * sigma
    hidden_grad = hg_ref[0]
    hidden_ref[0] = (silu * up_pre).astype(BF16)
    gg_ref[0] = (hidden_grad * up_pre * (sigma * (1.0 + gate_pre * (1.0 - sigma)))).astype(BF16)
    ug_ref[0] = (hidden_grad * silu).astype(BF16)


def weight_grad(order, source, act, groups, turned):
    cols = source.shape[2] // 8
    hid = act.shape[2]
    piece = (hid, cols) if turned else (cols, hid)

    def kernel(order_ref, src, act_ref, *outs):
        for e in range(2):
            side = act_ref[e].T if turned else act_ref[e]
            done = 0
            for out, count in zip(outs, groups):
                for n in range(count):
                    at = pl.ds(pl.multiple_of(order_ref[done] * cols, cols), cols)
                    rows = src[:, e * CAP : (e + 1) * CAP, at].reshape(ROWS, cols)
                    grad = mm(side, rows, 1, 0) if turned else mm(rows, side, 0, 0)
                    out[n, e] = grad.astype(BF16)
                    done += 1

    return pl.pallas_call(
        kernel,
        out_shape=tuple(jax.ShapeDtypeStruct((c, 2, *piece), BF16) for c in groups),
        in_specs=[smem(), vmem(), vmem()],
        out_specs=(vmem(),) * len(groups),
    )(order, source, act)


def expert_back_kernel(hidden_ref, down_ref, gg_ref, ug_ref, gate_ref, up_ref, out_ref):
    step = pl.program_id(0)
    shape = out_ref.shape

    @pl.when(step < 2)
    def _():
        out_ref[...] = mm(hidden_ref[0], down_ref[0], 1, 0).astype(BF16).reshape(shape)

    @pl.when(step >= 2)
    def _():
        total = mm(gg_ref[0], gate_ref[0], 1, 1) + mm(ug_ref[0], up_ref[0], 1, 1)
        out_ref[...] = total.astype(BF16).reshape(shape)


def pair_sum_kernel(keep_ref, got_ref, *outs):
    for n, out in enumerate(outs):
        out[...] = (keep_ref[n].astype(F32) + got_ref[n].astype(F32)).astype(out.dtype)


def mixed_kernel(back_ref, pick0_ref, pick1_ref, gates_ref, out_ref):
    back = back_ref[:, 0:2].reshape(EXPERTS * CAP, back_ref.shape[3])
    first = mm(pick0_ref[...], back, 0, 0) * gates_ref[:, 0:1]
    second = mm(pick1_ref[...], back, 0, 0) * gates_ref[:, 1:2]
    out_ref[...] = (first + second).astype(BF16)


def normed_grad_kernel(back_ref, pick0_ref, pick1_ref, out_ref):
    back = back_ref[:, 2:4].reshape(EXPERTS * CAP, back_ref.shape[3])
    pick = pick0_ref[...] + pick1_ref[...]
    out_ref[...] = mm(pick, back, 0, 0).astype(BF16)


def move_y(value, distance, keep=lambda hi, y: True):
    pairs = [
        (hi * 4 + y, hi * 4 + (y + distance) % 4)
        for hi in range(2)
        for y in range(4)
        if keep(hi, y)
    ]
    return lax.ppermute(value, "ctx", pairs)


def move_x(value, both=True):
    pairs = [(y, 4 + y) for y in range(4)]
    if both:
        pairs += [(4 + y, y) for y in range(4)]
    return lax.ppermute(value, "ctx", pairs)


def exchange(value):
    return lax.all_to_all(value, "exp", split_axis=0, concat_axis=0, tiled=True)


def step(queries, keys, values, gate_input, route_ids, route_gates, w_gate, w_up, w_down, out_grad):
    width = gate_input.shape[1]
    hid = w_gate.shape[2]
    ctx = lax.axis_index("ctx")
    hi, y = ctx // 4, ctx % 4
    full = jax.ShapeDtypeStruct
    down_x = [(n, 4 + n) for n in range(4)]
    up_x = [(4 + n, n) for n in range(4)]

    kv = jnp.stack([keys, values])
    lent_q = lax.ppermute(queries, "ctx", up_x)
    from_x = lax.ppermute(kv, "ctx", down_x)
    from_y1 = move_y(kv, 1, lambda hi, y: hi == 0 or y < 3)
    from_y2 = move_y(kv, 2, lambda hi, y: hi == 0 or y < 2)
    from_y3 = move_y(kv, 3, lambda hi, y: y == 0)
    from_xy = move_y(from_x, 3, lambda hi, y: hi == 1)
    from_xx = lax.ppermute(from_y2, "ctx", down_x)

    pick0, pick1, send_grads = pl.pallas_call(
        route_kernel,
        out_shape=(
            full((EXPERTS * CAP, TOK), BF16),
            full((EXPERTS * CAP, TOK), BF16),
            full((N_EXP, 2 * CAP, width), BF16),
        ),
        in_specs=[vmem()] * 3,
        out_specs=(vmem(),) * 3,
        name="route",
    )(route_ids.T, route_gates, out_grad)
    recv_grads = exchange(send_grads)

    flag = lambda *conds: jnp.stack([c.astype(jnp.int32) for c in conds])
    low, high = hi == 0, hi == 1
    acc = attend_own(queries, kv)
    lent = attend(flag(low, low), lent_q, [kv, from_y1], None, None, BF16)
    returned = lax.ppermute(lent, "ctx", down_x)
    acc = attend(flag(y >= 1, y >= 2, y >= 3), queries, [from_y1, from_y2, from_y3], acc, None, F32)
    attended = attend(flag(high, high), queries, [from_xx, from_xy], acc, returned, BF16)

    expert_block = pl.BlockSpec((N_EXP, CAP, width), lambda e: (0, e, 0))
    in_weight = pl.BlockSpec((1, width, hid), lambda e: (e, 0, 0))
    out_weight = pl.BlockSpec((1, hid, width), lambda e: (e, 0, 0))
    act_block = pl.BlockSpec((1, ROWS, hid), lambda e: (e, 0, 0))
    attended, recv_grads = lax.optimization_barrier((attended, recv_grads))
    token_heads = exchange(attended.reshape(N_EXP, TOK, HEAD_DIM))
    hidden_grad = pl.pallas_call(
        hidden_grad_kernel,
        grid=(2,),
        out_shape=full((2, ROWS, hid), F32),
        in_specs=[expert_block, out_weight],
        out_specs=act_block,
        name="hidden_grad",
    )(recv_grads, w_down)
    normed, send_inputs = pl.pallas_call(
        norm_kernel,
        out_shape=(full((TOK, width), BF16), full((N_EXP, 2 * CAP, width), BF16)),
        in_specs=[vmem()] * 4,
        out_specs=(vmem(),) * 2,
        name="norm",
    )(token_heads, gate_input, pick0, pick1)
    recv_inputs = exchange(send_inputs)

    act = full((2, ROWS, hid), BF16)
    hidden, gate_grad, up_grad = pl.pallas_call(
        expert_in_kernel,
        grid=(2,),
        out_shape=(act, act, act),
        in_specs=[expert_block, act_block, in_weight, in_weight],
        out_specs=(act_block,) * 3,
        name="expert_in",
    )(recv_inputs, hidden_grad, w_gate, w_up)

    turn = jnp.arange(4, dtype=jnp.int32)
    x_order = jnp.concatenate([(1 - hi) * 4 + (y + turn) % 4, hi * 4 + (y + turn) % 4])
    far = (turn + 1) % 4
    y_order = jnp.stack(
        [hi * 4 + (y + far) % 4, (1 - hi) * 4 + (y + far) % 4], axis=1
    ).reshape(8)
    up_send, up_keep = weight_grad(x_order, recv_inputs, up_grad, (4, 4), False)
    up_got = move_x(up_send)
    ga = weight_grad(y_order, recv_inputs, gate_grad, (2, 2, 2, 2), False)
    got_g = []
    for n in range(3):
        got_g.append(move_y(ga[n], n + 1))
    do = weight_grad(y_order, recv_grads, hidden, (2, 2, 2, 2), True)
    held = lax.optimization_barrier((*do[:3], *got_g))
    got_g = held[3:]
    got_d = []
    for n in range(3):
        got_d.append(move_y(held[n], n + 1))

    early = lambda shape: pl.BlockSpec((1, *shape), lambda n: (jnp.minimum(n, 1), 0, 0))
    late = lambda shape: pl.BlockSpec((1, *shape), lambda n: (jnp.maximum(n - 2, 0), 0, 0))
    expert_back = pl.pallas_call(
        expert_back_kernel,
        grid=(4,),
        out_shape=full((N_EXP, 4, CAP, width), BF16),
        in_specs=[
            early((ROWS, hid)),
            early((hid, width)),
            late((ROWS, hid)),
            late((ROWS, hid)),
            late((width, hid)),
            late((width, hid)),
        ],
        out_specs=pl.BlockSpec((N_EXP, 1, CAP, width), lambda n: (0, n, 0, 0)),
        name="expert_back",
    )(hidden, w_down, gate_grad, up_grad, w_gate, w_up)
    back = exchange(expert_back)

    token = full((TOK, width), BF16)
    mixed = pl.pallas_call(
        mixed_kernel, out_shape=token, in_specs=[vmem()] * 4, out_specs=vmem(), name="mixed"
    )(back, pick0, pick1, route_gates)
    normed_grad = pl.pallas_call(
        normed_grad_kernel, out_shape=token, in_specs=[vmem()] * 3, out_specs=vmem(), name="ngrad"
    )(back, pick0, pick1)

    wide = lambda v: v.astype(F32)

    def over_row(own, got):
        sums = wide(own) + wide(got[0]) + wide(got[1]) + wide(got[2])
        return sums[0], sums[1].astype(BF16)

    gate_part, gate_send = over_row(ga[3], got_g)
    gate_got = move_x(gate_send)
    gate_sum = (gate_part + wide(gate_got)).astype(BF16)
    quarter = up_keep.shape[1:]
    up_part, *up_rest = pl.pallas_call(
        pair_sum_kernel,
        out_shape=(full(quarter, F32),) + (full(quarter, BF16),) * 3,
        in_specs=[vmem()] * 2,
        out_specs=(vmem(),) * 4,
        name="pair_sum",
    )(up_keep, up_got)
    got_u = []
    for n in (1, 2, 3):
        got_u.append(move_y(up_rest[n - 1], n))
    up_sum = (up_part + wide(got_u[0]) + wide(got_u[1]) + wide(got_u[2])).astype(BF16)
    down_part, down_send = over_row(do[3], got_d)
    down_got = move_x(down_send)
    down_sum = (down_part + wide(down_got)).astype(BF16)
    return (normed, mixed, normed_grad, gate_sum, up_sum, down_sum)


def solution(mesh):
    in_specs = (
        P("ctx", "exp"),
        P("ctx", "exp"),
        P("ctx", "exp"),
        P(("ctx", "exp"), None),
        P(("ctx", "exp"), None),
        P(("ctx", "exp"), None),
        P("exp", None, None),
        P("exp", None, None),
        P("exp", None, None),
        P(("ctx", "exp"), None),
    )
    out_specs = (
        P(("ctx", "exp"), None),
        P(("ctx", "exp"), None),
        P(("ctx", "exp"), None),
        P("exp", "ctx", None),
        P("exp", "ctx", None),
        P("exp", None, "ctx"),
    )
    return jax.shard_map(step, mesh=mesh, in_specs=in_specs, out_specs=out_specs, check_vma=False)
```

```python
import math

import jax
import jax.numpy as jnp
from jax import lax
from jax.experimental import pallas as pl
from jax.experimental.pallas import tpu as pltpu
from jax.sharding import PartitionSpec as P


HEAD_DIM = 128
EXPERTS = 32
CAP = 16
N_EXP = 16
TOK = 128
ROWS = N_EXP * CAP
TQ = 512
TK = 256
F32 = jnp.float32
BF16 = jnp.bfloat16


def vmem():
    return pl.BlockSpec(memory_space=pltpu.VMEM)


def smem():
    return pl.BlockSpec(memory_space=pltpu.SMEM)


def mm(a, b, ca, cb):
    return lax.dot_general(a, b, (((ca,), (cb,)), ((), ())), preferred_element_type=F32)


def half_silu(scores):
    h = scores * (0.5 / math.sqrt(HEAD_DIM))
    return h + h * jnp.tanh(h)


def attend_tile(q, key_t, value, masked_from):
    w = half_silu(mm(q, key_t, 1, 0))
    if masked_from is not None:
        row = lax.broadcasted_iota(jnp.int32, w.shape, 0)
        col = lax.broadcasted_iota(jnp.int32, w.shape, 1)
        w = jnp.where(row >= col + masked_from, w, 0.0)
    return mm(w.astype(BF16), value, 1, 0)


def add_block(q_ref, turned, value, acc, rows):
    def q_step(i, carry):
        rows_i = pl.ds(pl.multiple_of(i * TQ, TQ), TQ)
        q = q_ref[rows_i, :]
        part = acc[rows_i, :]
        for j in range(rows // TK):
            rows_j = pl.ds(j * TK, TK)
            part = part + attend_tile(q, turned[:, rows_j], value[rows_j, :], None)
        acc[rows_i, :] = part
        return carry

    lax.fori_loop(0, rows // TQ, q_step, 0)


def attend_own(q, kv):
    rows = q.shape[0]

    def kernel(q_ref, kv, acc, turned):
        turned[...] = kv[0].T
        for i in range(rows // TQ):
            rows_i = pl.ds(i * TQ, TQ)
            part = jnp.zeros((TQ, HEAD_DIM), F32)
            for j in range((i + 1) * TQ // TK):
                rows_j = pl.ds(j * TK, TK)
                gap = j * TK - i * TQ
                part = part + attend_tile(
                    q_ref[rows_i, :], turned[:, rows_j], kv[1, rows_j, :], gap if gap >= 0 else None
                )
            acc[rows_i, :] = part

    return pl.pallas_call(
        kernel,
        out_shape=jax.ShapeDtypeStruct((rows, HEAD_DIM), F32),
        in_specs=[vmem()] * 2,
        out_specs=vmem(),
        scratch_shapes=[pltpu.VMEM((HEAD_DIM, rows), BF16)],
        name="attend_own",
    )(q, kv)


def attend(flags, q, kvs, base, out_type):
    rows = q.shape[0]
    count = len(kvs)

    def kernel(*refs):
        flags_ref, q_ref = refs[0], refs[1]
        kv_refs = refs[2 : 2 + count]
        base_ref = refs[2 + count]
        out, acc, turned, value = refs[-4:]
        acc[...] = base_ref[...]

        def one(n, carry):
            @pl.when(flags_ref[n] != 0)
            def _():
                for m, kv in enumerate(kv_refs):

                    @pl.when(n == m)
                    def _(kv=kv):
                        turned[...] = kv[0].T
                        value[...] = kv[1]

                add_block(q_ref, turned, value, acc, rows)

            return carry

        lax.fori_loop(0, count, one, 0)
        out[...] = acc[...].astype(out_type)

    return pl.pallas_call(
        kernel,
        out_shape=jax.ShapeDtypeStruct((rows, HEAD_DIM), out_type),
        in_specs=[smem()] + [vmem()] * (2 + count),
        out_specs=vmem(),
        scratch_shapes=[
            pltpu.VMEM((rows, HEAD_DIM), F32),
            pltpu.VMEM((HEAD_DIM, rows), BF16),
            pltpu.VMEM((rows, HEAD_DIM), BF16),
        ],
    )(flags, q, *kvs, base)


def route_kernel(ids_ref, gates_ref, grad_ref, pick0_ref, pick1_ref, send_ref):
    ids = ids_ref[...]
    expert = lax.broadcasted_iota(jnp.int32, (EXPERTS, TOK), 0)
    one0 = (expert == ids[0:1, :]).astype(F32)
    one1 = (expert == ids[1:2, :]).astype(F32)
    earlier = lax.broadcasted_iota(jnp.int32, (TOK, TOK), 0) < lax.broadcasted_iota(
        jnp.int32, (TOK, TOK), 1
    )
    counts = mm((one0 + one1).astype(BF16), earlier.astype(F32).astype(BF16), 1, 0)
    slot0 = jnp.sum(one0 * counts, axis=0, keepdims=True).astype(jnp.int32)
    slot1 = jnp.sum(one1 * (counts + one0), axis=0, keepdims=True).astype(jnp.int32)
    row = lax.broadcasted_iota(jnp.int32, (EXPERTS * CAP, TOK), 0)
    pick0 = (row == ids[0:1, :] * CAP + slot0).astype(F32).astype(BF16)
    pick1 = (row == ids[1:2, :] * CAP + slot1).astype(F32).astype(BF16)
    pick0_ref[...] = pick0
    pick1_ref[...] = pick1
    grad = grad_ref[...].astype(F32)
    scaled0 = (gates_ref[:, 0:1] * grad).astype(BF16)
    scaled1 = (gates_ref[:, 1:2] * grad).astype(BF16)
    sent = mm(pick0, scaled0, 1, 0) + mm(pick1, scaled1, 1, 0)
    send_ref[...] = sent.astype(BF16).reshape(send_ref.shape)


def norm_kernel(tok_ref, gate_ref, pick0_ref, pick1_ref, normed_ref, send_ref):
    heads = [tok_ref[h].astype(F32) for h in range(tok_ref.shape[0])]
    width = HEAD_DIM * len(heads)
    total = heads[0]
    for h in heads[1:]:
        total = total + h
    mean = jnp.sum(total, axis=1, keepdims=True) * (1.0 / width)
    squares = None
    for h in heads:
        c = h - mean
        squares = c * c if squares is None else squares + c * c
    variance = jnp.sum(squares, axis=1, keepdims=True) * (1.0 / width)
    scale = lax.rsqrt(variance + 1e-05)
    for n, h in enumerate(heads):
        cols = slice(n * HEAD_DIM, (n + 1) * HEAD_DIM)
        normed_ref[:, cols] = ((h - mean) * scale * gate_ref[:, cols].astype(F32)).astype(BF16)
    pick = pick0_ref[...] + pick1_ref[...]
    send_ref[...] = mm(pick, normed_ref[...], 1, 0).astype(BF16).reshape(send_ref.shape)


def hidden_grad_kernel(grad_ref, down_ref, out_ref):
    grads = grad_ref[...].reshape(ROWS, grad_ref.shape[2])
    out_ref[0] = mm(grads, down_ref[0], 1, 1)


def expert_in_kernel(in_ref, hg_ref, gate_ref, up_ref, hidden_ref, gg_ref, ug_ref):
    rows = in_ref[...].reshape(ROWS, in_ref.shape[2])
    gate_pre = mm(rows, gate_ref[0], 1, 0)
    up_pre = mm(rows, up_ref[0], 1, 0)
    sigma = jax.nn.sigmoid(gate_pre)
    silu = gate_pre * sigma
    hidden_grad = hg_ref[0]
    hidden_ref[0] = (silu * up_pre).astype(BF16)
    gg_ref[0] = (hidden_grad * up_pre * (sigma * (1.0 + gate_pre * (1.0 - sigma)))).astype(BF16)
    ug_ref[0] = (hidden_grad * silu).astype(BF16)


def weight_grad(order, source, act, groups, turned):
    cols = source.shape[2] // 8
    hid = act.shape[2]
    piece = (hid, cols) if turned else (cols, hid)

    def kernel(order_ref, src, act_ref, *outs):
        for e in range(2):
            side = act_ref[e].T if turned else act_ref[e]
            done = 0
            for out, count in zip(outs, groups):
                for n in range(count):
                    at = pl.ds(pl.multiple_of(order_ref[done] * cols, cols), cols)
                    rows = src[:, e * CAP : (e + 1) * CAP, at].reshape(ROWS, cols)
                    grad = mm(side, rows, 1, 0) if turned else mm(rows, side, 0, 0)
                    out[n, e] = grad.astype(BF16)
                    done += 1

    return pl.pallas_call(
        kernel,
        out_shape=tuple(jax.ShapeDtypeStruct((c, 2, *piece), BF16) for c in groups),
        in_specs=[smem(), vmem(), vmem()],
        out_specs=(vmem(),) * len(groups),
    )(order, source, act)


def expert_back_kernel(hidden_ref, down_ref, gg_ref, ug_ref, gate_ref, up_ref, out_ref):
    step = pl.program_id(0)
    shape = out_ref.shape

    @pl.when(step < 2)
    def _():
        out_ref[...] = mm(hidden_ref[0], down_ref[0], 1, 0).astype(BF16).reshape(shape)

    @pl.when(step >= 2)
    def _():
        total = mm(gg_ref[0], gate_ref[0], 1, 1) + mm(ug_ref[0], up_ref[0], 1, 1)
        out_ref[...] = total.astype(BF16).reshape(shape)


def pair_sum_kernel(keep_ref, got_ref, *outs):
    for n, out in enumerate(outs):
        out[...] = (keep_ref[n].astype(F32) + got_ref[n].astype(F32)).astype(out.dtype)


def mixed_kernel(back_ref, pick0_ref, pick1_ref, gates_ref, out_ref):
    back = back_ref[:, 0:2].reshape(EXPERTS * CAP, back_ref.shape[3])
    first = mm(pick0_ref[...], back, 0, 0) * gates_ref[:, 0:1]
    second = mm(pick1_ref[...], back, 0, 0) * gates_ref[:, 1:2]
    out_ref[...] = (first + second).astype(BF16)


def normed_grad_kernel(back_ref, pick0_ref, pick1_ref, out_ref):
    back = back_ref[:, 2:4].reshape(EXPERTS * CAP, back_ref.shape[3])
    pick = pick0_ref[...] + pick1_ref[...]
    out_ref[...] = mm(pick, back, 0, 0).astype(BF16)


def move_y(value, distance, keep=lambda hi, y: True):
    pairs = [
        (hi * 4 + y, hi * 4 + (y + distance) % 4)
        for hi in range(2)
        for y in range(4)
        if keep(hi, y)
    ]
    return lax.ppermute(value, "ctx", pairs)


def move_x(value, both=True):
    pairs = [(y, 4 + y) for y in range(4)]
    if both:
        pairs += [(4 + y, y) for y in range(4)]
    return lax.ppermute(value, "ctx", pairs)


def exchange(value):
    return lax.all_to_all(value, "exp", split_axis=0, concat_axis=0, tiled=True)


def step(queries, keys, values, gate_input, route_ids, route_gates, w_gate, w_up, w_down, out_grad):
    width = gate_input.shape[1]
    hid = w_gate.shape[2]
    ctx = lax.axis_index("ctx")
    hi, y = ctx // 4, ctx % 4
    full = jax.ShapeDtypeStruct
    down_x = [(n, 4 + n) for n in range(4)]
    in_high = lambda hi, y: hi == 1

    kv = jnp.stack([keys, values])
    from_y1 = move_y(kv, 1, lambda hi, y: y < 3)
    from_x = lax.ppermute(kv, "ctx", down_x)
    from_y2 = move_y(kv, 2, lambda hi, y: hi == 0 or y < 2)
    from_y3 = move_y(kv, 3, lambda hi, y: y == 0)
    from_xy1 = move_y(from_x, 1, in_high)
    from_xy3 = move_y(from_x, 3, in_high)
    from_xx = lax.ppermute(from_y2, "ctx", down_x)

    pick0, pick1, send_grads = pl.pallas_call(
        route_kernel,
        out_shape=(
            full((EXPERTS * CAP, TOK), BF16),
            full((EXPERTS * CAP, TOK), BF16),
            full((N_EXP, 2 * CAP, width), BF16),
        ),
        in_specs=[vmem()] * 3,
        out_specs=(vmem(),) * 3,
        name="route",
    )(route_ids.T, route_gates, out_grad)
    recv_grads = exchange(send_grads)

    flag = lambda *conds: jnp.stack([c.astype(jnp.int32) for c in conds])
    high = hi == 1
    acc = attend_own(queries, kv)
    stages = (
        (flag(y >= 1, high), [from_y1, from_x], F32),
        (flag(y >= 2, y >= 3), [from_y2, from_y3], F32),
        (flag(high, high), [from_xy1, from_xy3], F32),
        (flag(high), [from_xx], BF16),
    )
    for flags, blocks, kind in stages:
        acc = attend(flags, queries, blocks, acc, kind)
    attended = acc

    expert_block = pl.BlockSpec((N_EXP, CAP, width), lambda e: (0, e, 0))
    in_weight = pl.BlockSpec((1, width, hid), lambda e: (e, 0, 0))
    out_weight = pl.BlockSpec((1, hid, width), lambda e: (e, 0, 0))
    act_block = pl.BlockSpec((1, ROWS, hid), lambda e: (e, 0, 0))
    attended, recv_grads = lax.optimization_barrier((attended, recv_grads))
    token_heads = exchange(attended.reshape(N_EXP, TOK, HEAD_DIM))
    hidden_grad = pl.pallas_call(
        hidden_grad_kernel,
        grid=(2,),
        out_shape=full((2, ROWS, hid), F32),
        in_specs=[expert_block, out_weight],
        out_specs=act_block,
        name="hidden_grad",
    )(recv_grads, w_down)
    normed, send_inputs = pl.pallas_call(
        norm_kernel,
        out_shape=(full((TOK, width), BF16), full((N_EXP, 2 * CAP, width), BF16)),
        in_specs=[vmem()] * 4,
        out_specs=(vmem(),) * 2,
        name="norm",
    )(token_heads, gate_input, pick0, pick1)
    recv_inputs = exchange(send_inputs)

    act = full((2, ROWS, hid), BF16)
    hidden, gate_grad, up_grad = pl.pallas_call(
        expert_in_kernel,
        grid=(2,),
        out_shape=(act, act, act),
        in_specs=[expert_block, act_block, in_weight, in_weight],
        out_specs=(act_block,) * 3,
        name="expert_in",
    )(recv_inputs, hidden_grad, w_gate, w_up)

    turn = jnp.arange(4, dtype=jnp.int32)
    x_order = jnp.concatenate([(1 - hi) * 4 + (y + turn) % 4, hi * 4 + (y + turn) % 4])
    far = (turn + 1) % 4
    y_order = jnp.stack(
        [hi * 4 + (y + far) % 4, (1 - hi) * 4 + (y + far) % 4], axis=1
    ).reshape(8)
    ga = weight_grad(y_order, recv_inputs, gate_grad, (2, 2, 2, 2), False)
    got_g = []
    for n in range(3):
        got_g.append(move_y(ga[n], n + 1))
    up_send, up_keep = weight_grad(x_order, recv_inputs, up_grad, (4, 4), False)
    up_got = move_x(up_send)
    do = weight_grad(y_order, recv_grads, hidden, (2, 2, 2, 2), True)
    held = lax.optimization_barrier((*do[:3], *got_g))
    got_g = held[3:]
    got_d = []
    for n in range(3):
        got_d.append(move_y(held[n], n + 1))

    early = lambda shape: pl.BlockSpec((1, *shape), lambda n: (jnp.minimum(n, 1), 0, 0))
    late = lambda shape: pl.BlockSpec((1, *shape), lambda n: (jnp.maximum(n - 2, 0), 0, 0))
    expert_back = pl.pallas_call(
        expert_back_kernel,
        grid=(4,),
        out_shape=full((N_EXP, 4, CAP, width), BF16),
        in_specs=[
            early((ROWS, hid)),
            early((hid, width)),
            late((ROWS, hid)),
            late((ROWS, hid)),
            late((width, hid)),
            late((width, hid)),
        ],
        out_specs=pl.BlockSpec((N_EXP, 1, CAP, width), lambda n: (0, n, 0, 0)),
        name="expert_back",
    )(hidden, w_down, gate_grad, up_grad, w_gate, w_up)
    back = exchange(expert_back)

    token = full((TOK, width), BF16)
    mixed = pl.pallas_call(
        mixed_kernel, out_shape=token, in_specs=[vmem()] * 4, out_specs=vmem(), name="mixed"
    )(back, pick0, pick1, route_gates)
    normed_grad = pl.pallas_call(
        normed_grad_kernel, out_shape=token, in_specs=[vmem()] * 3, out_specs=vmem(), name="ngrad"
    )(back, pick0, pick1)

    wide = lambda v: v.astype(F32)

    def over_row(own, got):
        sums = wide(own) + wide(got[0]) + wide(got[1]) + wide(got[2])
        return sums[0], sums[1].astype(BF16)

    gate_part, gate_send = over_row(ga[3], got_g)
    gate_got = move_x(gate_send)
    gate_sum = (gate_part + wide(gate_got)).astype(BF16)
    quarter = up_keep.shape[1:]
    up_part, *up_rest = pl.pallas_call(
        pair_sum_kernel,
        out_shape=(full(quarter, F32),) + (full(quarter, BF16),) * 3,
        in_specs=[vmem()] * 2,
        out_specs=(vmem(),) * 4,
        name="pair_sum",
    )(up_keep, up_got)
    got_u = []
    for n in (1, 2, 3):
        got_u.append(move_y(up_rest[n - 1], n))
    up_sum = (up_part + wide(got_u[0]) + wide(got_u[1]) + wide(got_u[2])).astype(BF16)
    down_part, down_send = over_row(do[3], got_d)
    down_got = move_x(down_send)
    down_sum = (down_part + wide(down_got)).astype(BF16)
    return (normed, mixed, normed_grad, gate_sum, up_sum, down_sum)


def solution(mesh):
    in_specs = (
        P("ctx", "exp"),
        P("ctx", "exp"),
        P("ctx", "exp"),
        P(("ctx", "exp"), None),
        P(("ctx", "exp"), None),
        P(("ctx", "exp"), None),
        P("exp", None, None),
        P("exp", None, None),
        P("exp", None, None),
        P(("ctx", "exp"), None),
    )
    out_specs = (
        P(("ctx", "exp"), None),
        P(("ctx", "exp"), None),
        P(("ctx", "exp"), None),
        P("exp", "ctx", None),
        P("exp", "ctx", None),
        P("exp", None, "ctx"),
    )
    return jax.shard_map(step, mesh=mesh, in_specs=in_specs, out_specs=out_specs, check_vma=False)
```

```python
import math

import jax
import jax.numpy as jnp
import numpy as np
from jax import lax
from jax.experimental import pallas as pl
from jax.experimental.pallas import tpu as pltpu
from jax.sharding import PartitionSpec as P


HEAD_DIM = 128
EXPERTS = 32
CAP = 16
N_EXP = 16
TOK = 128
ROWS = N_EXP * CAP
TQ = 512
TK = 256
F32 = jnp.float32
BF16 = jnp.bfloat16


def vmem():
    return pl.BlockSpec(memory_space=pltpu.VMEM)


def smem():
    return pl.BlockSpec(memory_space=pltpu.SMEM)


def mm(a, b, ca, cb):
    return lax.dot_general(a, b, (((ca,), (cb,)), ((), ())), preferred_element_type=F32)


def half_silu(scores):
    h = scores * (0.5 / math.sqrt(HEAD_DIM))
    return h + h * jnp.tanh(h)


def attend_tile(q, key_t, value, masked_from):
    w = half_silu(mm(q, key_t, 1, 0))
    if masked_from is not None:
        row = lax.broadcasted_iota(jnp.int32, w.shape, 0)
        col = lax.broadcasted_iota(jnp.int32, w.shape, 1)
        w = jnp.where(row >= col + masked_from, w, 0.0)
    return mm(w.astype(BF16), value, 1, 0)


def add_block(q_ref, turned, value, acc, rows):
    def q_step(i, carry):
        rows_i = pl.ds(pl.multiple_of(i * TQ, TQ), TQ)
        q = q_ref[rows_i, :]
        part = acc[rows_i, :]
        for j in range(rows // TK):
            rows_j = pl.ds(j * TK, TK)
            part = part + attend_tile(q, turned[:, rows_j], value[rows_j, :], None)
        acc[rows_i, :] = part
        return carry

    lax.fori_loop(0, rows // TQ, q_step, 0)


def attend_own(q, kv):
    rows = q.shape[0]

    def kernel(q_ref, kv, acc, turned):
        turned[...] = kv[0].T
        for i in range(rows // TQ):
            rows_i = pl.ds(i * TQ, TQ)
            part = jnp.zeros((TQ, HEAD_DIM), F32)
            for j in range((i + 1) * TQ // TK):
                rows_j = pl.ds(j * TK, TK)
                gap = j * TK - i * TQ
                part = part + attend_tile(
                    q_ref[rows_i, :], turned[:, rows_j], kv[1, rows_j, :], gap if gap >= 0 else None
                )
            acc[rows_i, :] = part

    return pl.pallas_call(
        kernel,
        out_shape=jax.ShapeDtypeStruct((rows, HEAD_DIM), F32),
        in_specs=[vmem()] * 2,
        out_specs=vmem(),
        scratch_shapes=[pltpu.VMEM((HEAD_DIM, rows), BF16)],
        name="attend_own",
    )(q, kv)


def attend(table, offset, work, queries, kvs, bases, out_types):
    rows = queries[0].shape[-2]
    count = len(work)
    counts = (len(queries), len(kvs), sum(b is not None for b in bases), len(out_types))

    def kernel(*refs):
        flags_ref, refs = refs[0], refs[1:]
        groups = []
        for size in counts:
            groups.append(refs[:size])
            refs = refs[size:]
        q_refs, kv_refs, base_refs, outs = groups
        acc, q_all, turned, value = refs
        base_refs = list(base_refs)
        for n, q in enumerate(q_refs):
            q_all[n] = q[0] if len(q.shape) == 3 else q[...]
            if bases[n] is None:
                acc[n] = jnp.zeros(acc.shape[1:], F32)
            else:
                acc[n] = base_refs.pop(0)[...]

        def one(n, carry):
            @pl.when(flags_ref[offset + n] != 0)
            def _():
                side = flags_ref[offset + n] - 1
                for m, (_, source) in enumerate(work):

                    @pl.when(n == m)
                    def _(source=source):
                        turned[...] = kv_refs[source][0].T
                        value[...] = kv_refs[source][1]

                add_block(q_all.at[side], turned, value, acc.at[side], rows)

            return carry

        lax.fori_loop(0, count, one, 0)
        for n, out in enumerate(outs):
            out[...] = acc[n].astype(out.dtype)

    used = [b for b in bases if b is not None]
    return pl.pallas_call(
        kernel,
        out_shape=tuple(jax.ShapeDtypeStruct((rows, HEAD_DIM), t) for t in out_types),
        in_specs=[smem()] + [vmem()] * sum(counts[:3]),
        out_specs=(vmem(),) * len(out_types),
        scratch_shapes=[
            pltpu.VMEM((len(queries), rows, HEAD_DIM), F32),
            pltpu.VMEM((len(queries), rows, HEAD_DIM), BF16),
            pltpu.VMEM((HEAD_DIM, rows), BF16),
            pltpu.VMEM((rows, HEAD_DIM), BF16),
        ],
    )(table, *queries, *kvs, *used)


def route_kernel(ids_ref, gates_ref, grad_ref, pick0_ref, pick1_ref, send_ref):
    ids = ids_ref[...]
    expert = lax.broadcasted_iota(jnp.int32, (EXPERTS, TOK), 0)
    one0 = (expert == ids[0:1, :]).astype(F32)
    one1 = (expert == ids[1:2, :]).astype(F32)
    earlier = lax.broadcasted_iota(jnp.int32, (TOK, TOK), 0) < lax.broadcasted_iota(
        jnp.int32, (TOK, TOK), 1
    )
    counts = mm((one0 + one1).astype(BF16), earlier.astype(F32).astype(BF16), 1, 0)
    slot0 = jnp.sum(one0 * counts, axis=0, keepdims=True).astype(jnp.int32)
    slot1 = jnp.sum(one1 * (counts + one0), axis=0, keepdims=True).astype(jnp.int32)
    row = lax.broadcasted_iota(jnp.int32, (EXPERTS * CAP, TOK), 0)
    pick0 = (row == ids[0:1, :] * CAP + slot0).astype(F32).astype(BF16)
    pick1 = (row == ids[1:2, :] * CAP + slot1).astype(F32).astype(BF16)
    pick0_ref[...] = pick0
    pick1_ref[...] = pick1
    grad = grad_ref[...].astype(F32)
    scaled0 = (gates_ref[:, 0:1] * grad).astype(BF16)
    scaled1 = (gates_ref[:, 1:2] * grad).astype(BF16)
    sent = mm(pick0, scaled0, 1, 0) + mm(pick1, scaled1, 1, 0)
    send_ref[...] = sent.astype(BF16).reshape(send_ref.shape)


def norm_kernel(tok_ref, gate_ref, pick0_ref, pick1_ref, normed_ref, send_ref):
    heads = [tok_ref[h].astype(F32) for h in range(tok_ref.shape[0])]
    width = HEAD_DIM * len(heads)
    total = heads[0]
    for h in heads[1:]:
        total = total + h
    mean = jnp.sum(total, axis=1, keepdims=True) * (1.0 / width)
    squares = None
    for h in heads:
        c = h - mean
        squares = c * c if squares is None else squares + c * c
    variance = jnp.sum(squares, axis=1, keepdims=True) * (1.0 / width)
    scale = lax.rsqrt(variance + 1e-05)
    for n, h in enumerate(heads):
        cols = slice(n * HEAD_DIM, (n + 1) * HEAD_DIM)
        normed_ref[:, cols] = ((h - mean) * scale * gate_ref[:, cols].astype(F32)).astype(BF16)
    pick = pick0_ref[...] + pick1_ref[...]
    send_ref[...] = mm(pick, normed_ref[...], 1, 0).astype(BF16).reshape(send_ref.shape)


def hidden_grad_kernel(grad_ref, down_ref, out_ref):
    grads = grad_ref[...].reshape(ROWS, grad_ref.shape[2])
    out_ref[0] = mm(grads, down_ref[0], 1, 1)


def expert_in_kernel(in_ref, hg_ref, gate_ref, up_ref, hidden_ref, gg_ref, ug_ref):
    rows = in_ref[...].reshape(ROWS, in_ref.shape[2])
    gate_pre = mm(rows, gate_ref[0], 1, 0)
    up_pre = mm(rows, up_ref[0], 1, 0)
    sigma = jax.nn.sigmoid(gate_pre)
    silu = gate_pre * sigma
    hidden_grad = hg_ref[0]
    hidden_ref[0] = (silu * up_pre).astype(BF16)
    gg_ref[0] = (hidden_grad * up_pre * (sigma * (1.0 + gate_pre * (1.0 - sigma)))).astype(BF16)
    ug_ref[0] = (hidden_grad * silu).astype(BF16)


def weight_grad(table, offset, source, act, groups, turned):
    cols = source.shape[2] // 8
    hid = act.shape[2]
    piece = (hid, cols) if turned else (cols, hid)

    def kernel(order_ref, src, act_ref, *outs):
        for e in range(2):
            side = act_ref[e].T if turned else act_ref[e]
            done = 0
            for out, count in zip(outs, groups):
                for n in range(count):
                    at = pl.ds(pl.multiple_of(order_ref[offset + done] * cols, cols), cols)
                    rows = src[:, e * CAP : (e + 1) * CAP, at].reshape(ROWS, cols)
                    grad = mm(side, rows, 1, 0) if turned else mm(rows, side, 0, 0)
                    out[n, e] = grad.astype(BF16)
                    done += 1

    return pl.pallas_call(
        kernel,
        out_shape=tuple(jax.ShapeDtypeStruct((c, 2, *piece), BF16) for c in groups),
        in_specs=[smem(), vmem(), vmem()],
        out_specs=(vmem(),) * len(groups),
    )(table, source, act)


def expert_back_kernel(hidden_ref, down_ref, gg_ref, ug_ref, gate_ref, up_ref, out_ref):
    step = pl.program_id(0)
    shape = out_ref.shape

    @pl.when(step < 2)
    def _():
        out_ref[...] = mm(hidden_ref[0], down_ref[0], 1, 0).astype(BF16).reshape(shape)

    @pl.when(step >= 2)
    def _():
        total = mm(gg_ref[0], gate_ref[0], 1, 1) + mm(ug_ref[0], up_ref[0], 1, 1)
        out_ref[...] = total.astype(BF16).reshape(shape)


def pair_sum_kernel(keep_ref, got_ref, *outs):
    for n, out in enumerate(outs):
        out[...] = (keep_ref[n].astype(F32) + got_ref[n].astype(F32)).astype(out.dtype)


def mixed_kernel(back_ref, pick0_ref, pick1_ref, gates_ref, out_ref):
    back = back_ref[:, 0:2].reshape(EXPERTS * CAP, back_ref.shape[3])
    first = mm(pick0_ref[...], back, 0, 0) * gates_ref[:, 0:1]
    second = mm(pick1_ref[...], back, 0, 0) * gates_ref[:, 1:2]
    out_ref[...] = (first + second).astype(BF16)


def normed_grad_kernel(back_ref, pick0_ref, pick1_ref, out_ref):
    back = back_ref[:, 2:4].reshape(EXPERTS * CAP, back_ref.shape[3])
    pick = pick0_ref[...] + pick1_ref[...]
    out_ref[...] = mm(pick, back, 0, 0).astype(BF16)


def move_y(value, distance, keep=lambda hi, y: True):
    pairs = [
        (hi * 4 + y, hi * 4 + (y + distance) % 4)
        for hi in range(2)
        for y in range(4)
        if keep(hi, y)
    ]
    return lax.ppermute(value, "ctx", pairs)


def move_x(value, both=True):
    pairs = [(y, 4 + y) for y in range(4)]
    if both:
        pairs += [(4 + y, y) for y in range(4)]
    return lax.ppermute(value, "ctx", pairs)


def exchange(value):
    return lax.all_to_all(value, "exp", split_axis=0, concat_axis=0, tiled=True)


AT_NEAR, AT_FAR, AT_REST, AT_Y, AT_X = 0, 4, 6, 8, 16


def shard_table():
    lines = []
    for shard in range(8):
        hi, y = divmod(shard, 4)
        low, high = int(hi == 0), hi
        line = [2 * low, int(y >= 1), high, int(y >= 3), 2 * low, high, int(y >= 2), 0]
        for n in (1, 2, 3, 0):
            line += [hi * 4 + (y + n) % 4, (1 - hi) * 4 + (y + n) % 4]
        line += [(1 - hi) * 4 + (y + n) % 4 for n in range(4)]
        line += [hi * 4 + (y + n) % 4 for n in range(4)]
        lines.append(line)
    return np.asarray(lines, np.int32)


def step(queries, keys, values, gate_input, route_ids, route_gates, w_gate, w_up, w_down, out_grad):
    width = gate_input.shape[1]
    hid = w_gate.shape[2]
    ctx = lax.axis_index("ctx")
    full = jax.ShapeDtypeStruct
    down_x = [(n, 4 + n) for n in range(4)]
    table = lax.dynamic_index_in_dim(jnp.asarray(shard_table()), ctx, 0, keepdims=False)

    kv = jnp.stack([keys, values])
    from_y1 = move_y(kv, 1, lambda hi, y: hi == 0 or y < 3)
    from_x = move_x(jnp.where(ctx >= 4, queries[None], kv))
    from_y3 = move_y(kv, 3, lambda hi, y: y == 0)
    from_y2 = move_y(from_y1, 1, lambda hi, y: hi == 0 or y in (1, 2))
    from_xy3 = move_y(from_x, 3, lambda hi, y: hi == 1)

    pick0, pick1, send_grads = pl.pallas_call(
        route_kernel,
        out_shape=(
            full((EXPERTS * CAP, TOK), BF16),
            full((EXPERTS * CAP, TOK), BF16),
            full((N_EXP, 2 * CAP, width), BF16),
        ),
        in_specs=[vmem()] * 3,
        out_specs=(vmem(),) * 3,
        name="route",
    )(route_ids.T, route_gates, out_grad)
    recv_grads = exchange(send_grads)

    acc = attend_own(queries, kv)
    acc, lent = attend(
        table,
        AT_NEAR,
        ((1, 0), (0, 0), (0, 1), (0, 2)),
        [queries, from_x],
        [from_y1, from_x, from_y3],
        [acc, None],
        (F32, F32),
    )
    acc, lent = attend(
        table,
        AT_FAR,
        ((1, 0), (0, 1)),
        [queries, from_x],
        [from_y2, from_xy3],
        [acc, lent],
        (F32, BF16),
    )
    returned = lax.ppermute(lent, "ctx", down_x)
    (acc,) = attend(table, AT_REST, ((0, 0),), [queries], [from_y2], [acc], (F32,))
    attended = (acc + returned.astype(F32)).astype(BF16)

    expert_block = pl.BlockSpec((N_EXP, CAP, width), lambda e: (0, e, 0))
    in_weight = pl.BlockSpec((1, width, hid), lambda e: (e, 0, 0))
    out_weight = pl.BlockSpec((1, hid, width), lambda e: (e, 0, 0))
    act_block = pl.BlockSpec((1, ROWS, hid), lambda e: (e, 0, 0))
    attended, recv_grads = lax.optimization_barrier((attended, recv_grads))
    token_heads = exchange(attended.reshape(N_EXP, TOK, HEAD_DIM))
    hidden_grad = pl.pallas_call(
        hidden_grad_kernel,
        grid=(2,),
        out_shape=full((2, ROWS, hid), F32),
        in_specs=[expert_block, out_weight],
        out_specs=act_block,
        name="hidden_grad",
    )(recv_grads, w_down)
    normed, send_inputs = pl.pallas_call(
        norm_kernel,
        out_shape=(full((TOK, width), BF16), full((N_EXP, 2 * CAP, width), BF16)),
        in_specs=[vmem()] * 4,
        out_specs=(vmem(),) * 2,
        name="norm",
    )(token_heads, gate_input, pick0, pick1)
    recv_inputs = exchange(send_inputs)

    act = full((2, ROWS, hid), BF16)
    hidden, gate_grad, up_grad = pl.pallas_call(
        expert_in_kernel,
        grid=(2,),
        out_shape=(act, act, act),
        in_specs=[expert_block, act_block, in_weight, in_weight],
        out_specs=(act_block,) * 3,
        name="expert_in",
    )(recv_inputs, hidden_grad, w_gate, w_up)

    ga = weight_grad(table, AT_Y, recv_inputs, gate_grad, (2, 2, 2, 2), False)
    got_g = []
    for n in range(3):
        got_g.append(move_y(ga[n], n + 1))
    up_send, up_keep = weight_grad(table, AT_X, recv_inputs, up_grad, (4, 4), False)
    up_got = move_x(up_send)
    do = weight_grad(table, AT_Y, recv_grads, hidden, (2, 2, 2, 2), True)
    held = lax.optimization_barrier((*do[:3], *got_g))
    got_g = held[3:]
    got_d = []
    for n in range(3):
        got_d.append(move_y(held[n], n + 1))

    early = lambda shape: pl.BlockSpec((1, *shape), lambda n: (jnp.minimum(n, 1), 0, 0))
    late = lambda shape: pl.BlockSpec((1, *shape), lambda n: (jnp.maximum(n - 2, 0), 0, 0))
    expert_back = pl.pallas_call(
        expert_back_kernel,
        grid=(4,),
        out_shape=full((N_EXP, 4, CAP, width), BF16),
        in_specs=[
            early((ROWS, hid)),
            early((hid, width)),
            late((ROWS, hid)),
            late((ROWS, hid)),
            late((width, hid)),
            late((width, hid)),
        ],
        out_specs=pl.BlockSpec((N_EXP, 1, CAP, width), lambda n: (0, n, 0, 0)),
        name="expert_back",
    )(hidden, w_down, gate_grad, up_grad, w_gate, w_up)
    back = exchange(expert_back)

    token = full((TOK, width), BF16)
    mixed = pl.pallas_call(
        mixed_kernel, out_shape=token, in_specs=[vmem()] * 4, out_specs=vmem(), name="mixed"
    )(back, pick0, pick1, route_gates)
    normed_grad = pl.pallas_call(
        normed_grad_kernel, out_shape=token, in_specs=[vmem()] * 3, out_specs=vmem(), name="ngrad"
    )(back, pick0, pick1)

    wide = lambda v: v.astype(F32)

    def over_row(own, got):
        sums = wide(own) + wide(got[0]) + wide(got[1]) + wide(got[2])
        return sums[0], sums[1].astype(BF16)

    gate_part, gate_send = over_row(ga[3], got_g)
    gate_got = move_x(gate_send)
    quarter = up_keep.shape[1:]
    up_part, *up_rest = pl.pallas_call(
        pair_sum_kernel,
        out_shape=(full(quarter, F32),) + (full(quarter, BF16),) * 3,
        in_specs=[vmem()] * 2,
        out_specs=(vmem(),) * 4,
        name="pair_sum",
    )(up_keep, up_got)
    got_u = []
    for n in (1, 2, 3):
        got_u.append(move_y(up_rest[n - 1], n))
    mixed, normed_grad, gate_got, *got_u = lax.optimization_barrier(
        (mixed, normed_grad, gate_got, *got_u)
    )
    gate_sum = (gate_part + wide(gate_got)).astype(BF16)
    up_sum = (up_part + wide(got_u[0]) + wide(got_u[1]) + wide(got_u[2])).astype(BF16)
    down_part, down_send = over_row(do[3], got_d)
    down_got = move_x(down_send)
    down_sum = (down_part + wide(down_got)).astype(BF16)
    return (normed, mixed, normed_grad, gate_sum, up_sum, down_sum)


def solution(mesh):
    in_specs = (
        P("ctx", "exp"),
        P("ctx", "exp"),
        P("ctx", "exp"),
        P(("ctx", "exp"), None),
        P(("ctx", "exp"), None),
        P(("ctx", "exp"), None),
        P("exp", None, None),
        P("exp", None, None),
        P("exp", None, None),
        P(("ctx", "exp"), None),
    )
    out_specs = (
        P(("ctx", "exp"), None),
        P(("ctx", "exp"), None),
        P(("ctx", "exp"), None),
        P("exp", "ctx", None),
        P("exp", "ctx", None),
        P("exp", None, "ctx"),
    )
    return jax.shard_map(step, mesh=mesh, in_specs=in_specs, out_specs=out_specs, check_vma=False)
```

```python
import math

import jax
import jax.numpy as jnp
import numpy as np
from jax import lax
from jax.experimental import pallas as pl
from jax.experimental.pallas import tpu as pltpu
from jax.sharding import PartitionSpec as P


HEAD_DIM = 128
EXPERTS = 32
CAP = 16
N_EXP = 16
TOK = 128
ROWS = N_EXP * CAP
TQ = 512
TK = 256
F32 = jnp.float32
BF16 = jnp.bfloat16


def vmem():
    return pl.BlockSpec(memory_space=pltpu.VMEM)


def smem():
    return pl.BlockSpec(memory_space=pltpu.SMEM)


def mm(a, b, ca, cb):
    return lax.dot_general(a, b, (((ca,), (cb,)), ((), ())), preferred_element_type=F32)


def half_silu(scores):
    h = scores * (0.5 / math.sqrt(HEAD_DIM))
    return h + h * jnp.tanh(h)


def attend_tile(q, key_t, value, masked_from):
    w = half_silu(mm(q, key_t, 1, 0))
    if masked_from is not None:
        row = lax.broadcasted_iota(jnp.int32, w.shape, 0)
        col = lax.broadcasted_iota(jnp.int32, w.shape, 1)
        w = jnp.where(row >= col + masked_from, w, 0.0)
    return mm(w.astype(BF16), value, 1, 0)


def add_block(q_ref, turned, value, acc, rows):
    def q_step(i, carry):
        rows_i = pl.ds(pl.multiple_of(i * TQ, TQ), TQ)
        q = q_ref[rows_i, :]
        part = acc[rows_i, :]
        for j in range(rows // TK):
            rows_j = pl.ds(j * TK, TK)
            part = part + attend_tile(q, turned[:, rows_j], value[rows_j, :], None)
        acc[rows_i, :] = part
        return carry

    lax.fori_loop(0, rows // TQ, q_step, 0)


def attend_own(q, kv):
    rows = q.shape[0]

    def kernel(q_ref, kv, acc, turned):
        turned[...] = kv[0].T
        for i in range(rows // TQ):
            rows_i = pl.ds(i * TQ, TQ)
            part = jnp.zeros((TQ, HEAD_DIM), F32)
            for j in range((i + 1) * TQ // TK):
                rows_j = pl.ds(j * TK, TK)
                gap = j * TK - i * TQ
                part = part + attend_tile(
                    q_ref[rows_i, :], turned[:, rows_j], kv[1, rows_j, :], gap if gap >= 0 else None
                )
            acc[rows_i, :] = part

    return pl.pallas_call(
        kernel,
        out_shape=jax.ShapeDtypeStruct((rows, HEAD_DIM), F32),
        in_specs=[vmem()] * 2,
        out_specs=vmem(),
        scratch_shapes=[pltpu.VMEM((HEAD_DIM, rows), BF16)],
        name="attend_own",
    )(q, kv)


def attend(table, offset, work, queries, kvs, bases, out_types):
    rows = queries[0].shape[-2]
    count = len(work)
    counts = (len(queries), len(kvs), sum(b is not None for b in bases), len(out_types))

    def kernel(*refs):
        flags_ref, refs = refs[0], refs[1:]
        groups = []
        for size in counts:
            groups.append(refs[:size])
            refs = refs[size:]
        q_refs, kv_refs, base_refs, outs = groups
        acc, q_all, turned, value = refs
        base_refs = list(base_refs)
        for n, q in enumerate(q_refs):
            q_all[n] = q[0] if len(q.shape) == 3 else q[...]
            if bases[n] is None:
                acc[n] = jnp.zeros(acc.shape[1:], F32)
            else:
                acc[n] = base_refs.pop(0)[...]

        def one(n, carry):
            @pl.when(flags_ref[offset + n] != 0)
            def _():
                side = flags_ref[offset + n] - 1
                for m, (_, source) in enumerate(work):

                    @pl.when(n == m)
                    def _(source=source):
                        turned[...] = kv_refs[source][0].T
                        value[...] = kv_refs[source][1]

                add_block(q_all.at[side], turned, value, acc.at[side], rows)

            return carry

        lax.fori_loop(0, count, one, 0)
        for n, out in enumerate(outs):
            out[...] = acc[n].astype(out.dtype)

    used = [b for b in bases if b is not None]
    return pl.pallas_call(
        kernel,
        out_shape=tuple(jax.ShapeDtypeStruct((rows, HEAD_DIM), t) for t in out_types),
        in_specs=[smem()] + [vmem()] * sum(counts[:3]),
        out_specs=(vmem(),) * len(out_types),
        scratch_shapes=[
            pltpu.VMEM((len(queries), rows, HEAD_DIM), F32),
            pltpu.VMEM((len(queries), rows, HEAD_DIM), BF16),
            pltpu.VMEM((HEAD_DIM, rows), BF16),
            pltpu.VMEM((rows, HEAD_DIM), BF16),
        ],
    )(table, *queries, *kvs, *used)


def route_kernel(ids_ref, gates_ref, grad_ref, pick0_ref, pick1_ref, send_ref):
    ids = ids_ref[...]
    expert = lax.broadcasted_iota(jnp.int32, (EXPERTS, TOK), 0)
    one0 = (expert == ids[0:1, :]).astype(F32)
    one1 = (expert == ids[1:2, :]).astype(F32)
    earlier = lax.broadcasted_iota(jnp.int32, (TOK, TOK), 0) < lax.broadcasted_iota(
        jnp.int32, (TOK, TOK), 1
    )
    counts = mm((one0 + one1).astype(BF16), earlier.astype(F32).astype(BF16), 1, 0)
    slot0 = jnp.sum(one0 * counts, axis=0, keepdims=True).astype(jnp.int32)
    slot1 = jnp.sum(one1 * (counts + one0), axis=0, keepdims=True).astype(jnp.int32)
    row = lax.broadcasted_iota(jnp.int32, (EXPERTS * CAP, TOK), 0)
    pick0 = (row == ids[0:1, :] * CAP + slot0).astype(F32).astype(BF16)
    pick1 = (row == ids[1:2, :] * CAP + slot1).astype(F32).astype(BF16)
    pick0_ref[...] = pick0
    pick1_ref[...] = pick1
    grad = grad_ref[...].astype(F32)
    scaled0 = (gates_ref[:, 0:1] * grad).astype(BF16)
    scaled1 = (gates_ref[:, 1:2] * grad).astype(BF16)
    sent = mm(pick0, scaled0, 1, 0) + mm(pick1, scaled1, 1, 0)
    send_ref[...] = sent.astype(BF16).reshape(send_ref.shape)


def norm_kernel(tok_ref, gate_ref, pick0_ref, pick1_ref, normed_ref, send_ref):
    heads = [tok_ref[h].astype(F32) for h in range(tok_ref.shape[0])]
    width = HEAD_DIM * len(heads)
    total = heads[0]
    for h in heads[1:]:
        total = total + h
    mean = jnp.sum(total, axis=1, keepdims=True) * (1.0 / width)
    squares = None
    for h in heads:
        c = h - mean
        squares = c * c if squares is None else squares + c * c
    variance = jnp.sum(squares, axis=1, keepdims=True) * (1.0 / width)
    scale = lax.rsqrt(variance + 1e-05)
    for n, h in enumerate(heads):
        cols = slice(n * HEAD_DIM, (n + 1) * HEAD_DIM)
        normed_ref[:, cols] = ((h - mean) * scale * gate_ref[:, cols].astype(F32)).astype(BF16)
    pick = pick0_ref[...] + pick1_ref[...]
    send_ref[...] = mm(pick, normed_ref[...], 1, 0).astype(BF16).reshape(send_ref.shape)


def hidden_grad_kernel(grad_ref, down_ref, out_ref):
    grads = grad_ref[...].reshape(ROWS, grad_ref.shape[2])
    out_ref[0] = mm(grads, down_ref[0], 1, 1)


def expert_in_kernel(in_ref, hg_ref, gate_ref, up_ref, hidden_ref, gg_ref, ug_ref):
    rows = in_ref[...].reshape(ROWS, in_ref.shape[2])
    gate_pre = mm(rows, gate_ref[0], 1, 0)
    up_pre = mm(rows, up_ref[0], 1, 0)
    sigma = jax.nn.sigmoid(gate_pre)
    silu = gate_pre * sigma
    hidden_grad = hg_ref[0]
    hidden_ref[0] = (silu * up_pre).astype(BF16)
    gg_ref[0] = (hidden_grad * up_pre * (sigma * (1.0 + gate_pre * (1.0 - sigma)))).astype(BF16)
    ug_ref[0] = (hidden_grad * silu).astype(BF16)


def weight_grad(table, offset, source, act, groups, turned):
    cols = source.shape[2] // 8
    hid = act.shape[2]
    piece = (hid, cols) if turned else (cols, hid)

    def kernel(order_ref, src, act_ref, *outs):
        sides = [act_ref[e].T if turned else act_ref[e] for e in range(2)]
        for out, (first, count, experts) in zip(outs, groups):
            for n in range(count):
                owner = order_ref[offset + first + n]
                at = pl.ds(pl.multiple_of(owner * cols, cols), cols)
                for m, e in enumerate(experts):
                    rows = src[:, e * CAP : (e + 1) * CAP, at].reshape(ROWS, cols)
                    side = sides[e]
                    grad = mm(side, rows, 1, 0) if turned else mm(rows, side, 0, 0)
                    out[n, m] = grad.astype(BF16)

    return pl.pallas_call(
        kernel,
        out_shape=tuple(jax.ShapeDtypeStruct((c, len(x), *piece), BF16) for _, c, x in groups),
        in_specs=[smem(), vmem(), vmem()],
        out_specs=(vmem(),) * len(groups),
    )(table, source, act)


def relay_kernel(near1_ref, far1_ref, near3_ref, far3_ref, out1_ref, out3_ref):
    out1_ref[...] = (near1_ref[...].astype(F32) + far1_ref[...].astype(F32)).astype(BF16)
    out3_ref[...] = (near3_ref[...].astype(F32) + far3_ref[...].astype(F32)).astype(BF16)


def row_sum_kernel(own_ref, a1_ref, a3_ref, b1_ref, b3_ref, keep_ref, send_ref):
    for e, (one, three) in enumerate(((a1_ref, a3_ref), (b1_ref, b3_ref))):
        for n, out in enumerate((keep_ref, send_ref)):
            total = own_ref[n, e].astype(F32) + one[n, 0].astype(F32) + three[n, 0].astype(F32)
            out[e] = total.astype(out.dtype)


def expert_back_kernel(hidden_ref, down_ref, gg_ref, ug_ref, gate_ref, up_ref, out_ref):
    step = pl.program_id(0)
    shape = out_ref.shape

    @pl.when(step < 2)
    def _():
        out_ref[...] = mm(hidden_ref[0], down_ref[0], 1, 0).astype(BF16).reshape(shape)

    @pl.when(step >= 2)
    def _():
        total = mm(gg_ref[0], gate_ref[0], 1, 1) + mm(ug_ref[0], up_ref[0], 1, 1)
        out_ref[...] = total.astype(BF16).reshape(shape)


def pair_sum_kernel(keep_ref, got_ref, *outs):
    for n, out in enumerate(outs):
        out[...] = (keep_ref[n].astype(F32) + got_ref[n].astype(F32)).astype(out.dtype)


def mixed_kernel(back_ref, pick0_ref, pick1_ref, gates_ref, out_ref):
    back = back_ref[:, 0:2].reshape(EXPERTS * CAP, back_ref.shape[3])
    first = mm(pick0_ref[...], back, 0, 0) * gates_ref[:, 0:1]
    second = mm(pick1_ref[...], back, 0, 0) * gates_ref[:, 1:2]
    out_ref[...] = (first + second).astype(BF16)


def normed_grad_kernel(back_ref, pick0_ref, pick1_ref, out_ref):
    back = back_ref[:, 2:4].reshape(EXPERTS * CAP, back_ref.shape[3])
    pick = pick0_ref[...] + pick1_ref[...]
    out_ref[...] = mm(pick, back, 0, 0).astype(BF16)


def move_y(value, distance, keep=lambda hi, y: True):
    pairs = [
        (hi * 4 + y, hi * 4 + (y + distance) % 4)
        for hi in range(2)
        for y in range(4)
        if keep(hi, y)
    ]
    return lax.ppermute(value, "ctx", pairs)


def move_x(value, both=True):
    pairs = [(y, 4 + y) for y in range(4)]
    if both:
        pairs += [(4 + y, y) for y in range(4)]
    return lax.ppermute(value, "ctx", pairs)


def along_row(pieces):
    one_a, one_b, two_a, two_b, three_a, three_b, _ = pieces
    far1 = move_y(two_a, 1)
    far3 = move_y(two_b, 3)
    b1 = move_y(one_b, 1)
    a3 = move_y(three_a, 3)
    both1, both3 = pl.pallas_call(
        relay_kernel,
        out_shape=(
            jax.ShapeDtypeStruct(one_a.shape, BF16),
            jax.ShapeDtypeStruct(one_a.shape, BF16),
        ),
        in_specs=[vmem()] * 4,
        out_specs=(vmem(),) * 2,
        name="relay",
    )(one_a, far1, three_b, far3)
    a1 = move_y(both1, 1)
    b3 = move_y(both3, 3)
    return a1, a3, b1, b3


def exchange(value):
    return lax.all_to_all(value, "exp", split_axis=0, concat_axis=0, tiled=True)


ROW_GROUPS = tuple((n, 2, (e,)) for n in (0, 2, 4) for e in (0, 1)) + ((6, 2, (0, 1)),)
AT_NEAR, AT_FAR, AT_REST, AT_Y, AT_X = 0, 4, 6, 8, 16


def shard_table():
    lines = []
    for shard in range(8):
        hi, y = divmod(shard, 4)
        low, high = int(hi == 0), hi
        line = [2 * low, int(y >= 1), high, int(y >= 3), 2 * low, high, int(y >= 2), 0]
        for n in (1, 2, 3, 0):
            line += [hi * 4 + (y + n) % 4, (1 - hi) * 4 + (y + n) % 4]
        line += [(1 - hi) * 4 + (y + n) % 4 for n in range(4)]
        line += [hi * 4 + (y + n) % 4 for n in range(4)]
        lines.append(line)
    return np.asarray(lines, np.int32)


def step(queries, keys, values, gate_input, route_ids, route_gates, w_gate, w_up, w_down, out_grad):
    width = gate_input.shape[1]
    hid = w_gate.shape[2]
    ctx = lax.axis_index("ctx")
    full = jax.ShapeDtypeStruct
    down_x = [(n, 4 + n) for n in range(4)]
    table = lax.dynamic_index_in_dim(jnp.asarray(shard_table()), ctx, 0, keepdims=False)

    kv = jnp.stack([keys, values])
    from_y1 = move_y(kv, 1, lambda hi, y: hi == 0 or y < 3)
    from_x = move_x(jnp.where(ctx >= 4, queries[None], kv))
    from_y3 = move_y(kv, 3, lambda hi, y: y == 0)
    from_y2 = move_y(from_y1, 1, lambda hi, y: hi == 0 or y in (1, 2))
    from_xy3 = move_y(from_x, 3, lambda hi, y: hi == 1)

    pick0, pick1, send_grads = pl.pallas_call(
        route_kernel,
        out_shape=(
            full((EXPERTS * CAP, TOK), BF16),
            full((EXPERTS * CAP, TOK), BF16),
            full((N_EXP, 2 * CAP, width), BF16),
        ),
        in_specs=[vmem()] * 3,
        out_specs=(vmem(),) * 3,
        name="route",
    )(route_ids.T, route_gates, out_grad)
    recv_grads = exchange(send_grads)

    acc = attend_own(queries, kv)
    acc, lent = attend(
        table,
        AT_NEAR,
        ((1, 0), (0, 0), (0, 1), (0, 2)),
        [queries, from_x],
        [from_y1, from_x, from_y3],
        [acc, None],
        (F32, F32),
    )
    acc, lent = attend(
        table,
        AT_FAR,
        ((1, 0), (0, 1)),
        [queries, from_x],
        [from_y2, from_xy3],
        [acc, lent],
        (F32, BF16),
    )
    returned = lax.ppermute(lent, "ctx", down_x)
    (acc,) = attend(table, AT_REST, ((0, 0),), [queries], [from_y2], [acc], (F32,))
    attended = (acc + returned.astype(F32)).astype(BF16)

    expert_block = pl.BlockSpec((N_EXP, CAP, width), lambda e: (0, e, 0))
    in_weight = pl.BlockSpec((1, width, hid), lambda e: (e, 0, 0))
    out_weight = pl.BlockSpec((1, hid, width), lambda e: (e, 0, 0))
    act_block = pl.BlockSpec((1, ROWS, hid), lambda e: (e, 0, 0))
    attended, recv_grads = lax.optimization_barrier((attended, recv_grads))
    token_heads = exchange(attended.reshape(N_EXP, TOK, HEAD_DIM))
    hidden_grad = pl.pallas_call(
        hidden_grad_kernel,
        grid=(2,),
        out_shape=full((2, ROWS, hid), F32),
        in_specs=[expert_block, out_weight],
        out_specs=act_block,
        name="hidden_grad",
    )(recv_grads, w_down)
    normed, send_inputs = pl.pallas_call(
        norm_kernel,
        out_shape=(full((TOK, width), BF16), full((N_EXP, 2 * CAP, width), BF16)),
        in_specs=[vmem()] * 4,
        out_specs=(vmem(),) * 2,
        name="norm",
    )(token_heads, gate_input, pick0, pick1)
    recv_inputs = exchange(send_inputs)

    act = full((2, ROWS, hid), BF16)
    hidden, gate_grad, up_grad = pl.pallas_call(
        expert_in_kernel,
        grid=(2,),
        out_shape=(act, act, act),
        in_specs=[expert_block, act_block, in_weight, in_weight],
        out_specs=(act_block,) * 3,
        name="expert_in",
    )(recv_inputs, hidden_grad, w_gate, w_up)

    ga = weight_grad(table, AT_Y, recv_inputs, gate_grad, ROW_GROUPS, False)
    got_g = along_row(ga)
    up_send, up_keep, *ua = weight_grad(
        table,
        0,
        recv_inputs,
        up_grad,
        ((AT_X, 4, (0,)), (AT_X + 4, 4, (0,))) + tuple((AT_Y + n, 2, (1,)) for n in (0, 2, 4, 6)),
        False,
    )
    up_got = move_x(up_send)
    do = weight_grad(table, AT_Y, recv_grads, hidden, ROW_GROUPS, True)
    got_d = along_row(do)
    got_a = []
    for n in range(3):
        got_a.append(move_y(ua[n], n + 1))
    early = lambda shape: pl.BlockSpec((1, *shape), lambda n: (jnp.minimum(n, 1), 0, 0))
    late = lambda shape: pl.BlockSpec((1, *shape), lambda n: (jnp.maximum(n - 2, 0), 0, 0))
    expert_back = pl.pallas_call(
        expert_back_kernel,
        grid=(4,),
        out_shape=full((N_EXP, 4, CAP, width), BF16),
        in_specs=[
            early((ROWS, hid)),
            early((hid, width)),
            late((ROWS, hid)),
            late((ROWS, hid)),
            late((width, hid)),
            late((width, hid)),
        ],
        out_specs=pl.BlockSpec((N_EXP, 1, CAP, width), lambda n: (0, n, 0, 0)),
        name="expert_back",
    )(hidden, w_down, gate_grad, up_grad, w_gate, w_up)
    back = exchange(expert_back)

    token = full((TOK, width), BF16)
    mixed = pl.pallas_call(
        mixed_kernel, out_shape=token, in_specs=[vmem()] * 4, out_specs=vmem(), name="mixed"
    )(back, pick0, pick1, route_gates)
    normed_grad = pl.pallas_call(
        normed_grad_kernel, out_shape=token, in_specs=[vmem()] * 3, out_specs=vmem(), name="ngrad"
    )(back, pick0, pick1)

    wide = lambda v: v.astype(F32)

    def over_row(own, got):
        shape = own.shape[1:]
        return pl.pallas_call(
            row_sum_kernel,
            out_shape=(full(shape, F32), full(shape, BF16)),
            in_specs=[vmem()] * 5,
            out_specs=(vmem(),) * 2,
            name="row_sum",
        )(own, *got)

    gate_part, gate_send = over_row(ga[6], got_g)
    gate_got = move_x(gate_send)
    sums = wide(ua[3]) + wide(got_a[0]) + wide(got_a[1]) + wide(got_a[2])
    got_ax = move_x(sums[1].astype(BF16))
    quarter = up_keep.shape[1:]
    up_part, *up_rest = pl.pallas_call(
        pair_sum_kernel,
        out_shape=(full(quarter, F32),) + (full(quarter, BF16),) * 3,
        in_specs=[vmem()] * 2,
        out_specs=(vmem(),) * 4,
        name="pair_sum",
    )(up_keep, up_got)
    got_u = []
    for n in (1, 2, 3):
        got_u.append(move_y(up_rest[n - 1], n))
    mixed, normed_grad, gate_got, *got_u = lax.optimization_barrier(
        (mixed, normed_grad, gate_got, *got_u)
    )
    gate_sum = (gate_part + wide(gate_got)).astype(BF16)
    up_first = (up_part + wide(got_u[0]) + wide(got_u[1]) + wide(got_u[2])).astype(BF16)
    up_last = (sums[0] + wide(got_ax)).astype(BF16)
    up_sum = jnp.concatenate([up_first, up_last])
    down_part, down_send = over_row(do[6], got_d)
    down_got = move_x(down_send)
    down_sum = (down_part + wide(down_got)).astype(BF16)
    return (normed, mixed, normed_grad, gate_sum, up_sum, down_sum)


def solution(mesh):
    in_specs = (
        P("ctx", "exp"),
        P("ctx", "exp"),
        P("ctx", "exp"),
        P(("ctx", "exp"), None),
        P(("ctx", "exp"), None),
        P(("ctx", "exp"), None),
        P("exp", None, None),
        P("exp", None, None),
        P("exp", None, None),
        P(("ctx", "exp"), None),
    )
    out_specs = (
        P(("ctx", "exp"), None),
        P(("ctx", "exp"), None),
        P(("ctx", "exp"), None),
        P("exp", "ctx", None),
        P("exp", "ctx", None),
        P("exp", None, "ctx"),
    )
    return jax.shard_map(step, mesh=mesh, in_specs=in_specs, out_specs=out_specs, check_vma=False)
```

```python
import math

import jax
import jax.numpy as jnp
import numpy as np
from jax import lax
from jax.experimental import pallas as pl
from jax.experimental.pallas import tpu as pltpu
from jax.sharding import PartitionSpec as P


HEAD_DIM = 128
EXPERTS = 32
CAP = 16
N_EXP = 16
TOK = 128
ROWS = N_EXP * CAP
TQ = 512
TK = 256
F32 = jnp.float32
BF16 = jnp.bfloat16


def vmem():
    return pl.BlockSpec(memory_space=pltpu.VMEM)


def smem():
    return pl.BlockSpec(memory_space=pltpu.SMEM)


def mm(a, b, ca, cb):
    return lax.dot_general(a, b, (((ca,), (cb,)), ((), ())), preferred_element_type=F32)


def half_silu(scores):
    h = scores * (0.5 / math.sqrt(HEAD_DIM))
    return h + h * jnp.tanh(h)


def attend_tile(q, key_t, value, masked_from):
    w = half_silu(mm(q, key_t, 1, 0))
    if masked_from is not None:
        row = lax.broadcasted_iota(jnp.int32, w.shape, 0)
        col = lax.broadcasted_iota(jnp.int32, w.shape, 1)
        w = jnp.where(row >= col + masked_from, w, 0.0)
    return mm(w.astype(BF16), value, 1, 0)


def add_block(q_ref, turned, value, acc, rows):
    def q_step(i, carry):
        rows_i = pl.ds(pl.multiple_of(i * TQ, TQ), TQ)
        q = q_ref[rows_i, :]
        part = acc[rows_i, :]
        for j in range(rows // TK):
            rows_j = pl.ds(j * TK, TK)
            part = part + attend_tile(q, turned[:, rows_j], value[rows_j, :], None)
        acc[rows_i, :] = part
        return carry

    lax.fori_loop(0, rows // TQ, q_step, 0)


def attend_own(q, kv):
    rows = q.shape[0]

    def kernel(q_ref, kv, acc, turned):
        turned[...] = kv[0].T
        for i in range(rows // TQ):
            rows_i = pl.ds(i * TQ, TQ)
            part = jnp.zeros((TQ, HEAD_DIM), F32)
            for j in range((i + 1) * TQ // TK):
                rows_j = pl.ds(j * TK, TK)
                gap = j * TK - i * TQ
                part = part + attend_tile(
                    q_ref[rows_i, :], turned[:, rows_j], kv[1, rows_j, :], gap if gap >= 0 else None
                )
            acc[rows_i, :] = part

    return pl.pallas_call(
        kernel,
        out_shape=jax.ShapeDtypeStruct((rows, HEAD_DIM), F32),
        in_specs=[vmem()] * 2,
        out_specs=vmem(),
        scratch_shapes=[pltpu.VMEM((HEAD_DIM, rows), BF16)],
        name="attend_own",
    )(q, kv)


def attend(table, offset, work, queries, kvs, bases, out_types):
    rows = queries[0].shape[-2]
    count = len(work)
    counts = (len(queries), len(kvs), sum(b is not None for b in bases), len(out_types))

    def kernel(*refs):
        flags_ref, refs = refs[0], refs[1:]
        groups = []
        for size in counts:
            groups.append(refs[:size])
            refs = refs[size:]
        q_refs, kv_refs, base_refs, outs = groups
        acc, q_all, turned, value = refs
        base_refs = list(base_refs)
        for n, q in enumerate(q_refs):
            q_all[n] = q[0] if len(q.shape) == 3 else q[...]
            if bases[n] is None:
                acc[n] = jnp.zeros(acc.shape[1:], F32)
            else:
                acc[n] = base_refs.pop(0)[...]

        def one(n, carry):
            @pl.when(flags_ref[offset + n] != 0)
            def _():
                side = flags_ref[offset + n] - 1
                for m, (_, source) in enumerate(work):

                    @pl.when(n == m)
                    def _(source=source):
                        turned[...] = kv_refs[source][0].T
                        value[...] = kv_refs[source][1]

                add_block(q_all.at[side], turned, value, acc.at[side], rows)

            return carry

        lax.fori_loop(0, count, one, 0)
        for n, out in enumerate(outs):
            out[...] = acc[n].astype(out.dtype)

    used = [b for b in bases if b is not None]
    return pl.pallas_call(
        kernel,
        out_shape=tuple(jax.ShapeDtypeStruct((rows, HEAD_DIM), t) for t in out_types),
        in_specs=[smem()] + [vmem()] * sum(counts[:3]),
        out_specs=(vmem(),) * len(out_types),
        scratch_shapes=[
            pltpu.VMEM((len(queries), rows, HEAD_DIM), F32),
            pltpu.VMEM((len(queries), rows, HEAD_DIM), BF16),
            pltpu.VMEM((HEAD_DIM, rows), BF16),
            pltpu.VMEM((rows, HEAD_DIM), BF16),
        ],
    )(table, *queries, *kvs, *used)


def route_kernel(ids_ref, gates_ref, grad_ref, pick0_ref, pick1_ref, send_ref):
    ids = ids_ref[...]
    expert = lax.broadcasted_iota(jnp.int32, (EXPERTS, TOK), 0)
    one0 = (expert == ids[0:1, :]).astype(F32)
    one1 = (expert == ids[1:2, :]).astype(F32)
    earlier = lax.broadcasted_iota(jnp.int32, (TOK, TOK), 0) < lax.broadcasted_iota(
        jnp.int32, (TOK, TOK), 1
    )
    counts = mm((one0 + one1).astype(BF16), earlier.astype(F32).astype(BF16), 1, 0)
    slot0 = jnp.sum(one0 * counts, axis=0, keepdims=True).astype(jnp.int32)
    slot1 = jnp.sum(one1 * (counts + one0), axis=0, keepdims=True).astype(jnp.int32)
    row = lax.broadcasted_iota(jnp.int32, (EXPERTS * CAP, TOK), 0)
    pick0 = (row == ids[0:1, :] * CAP + slot0).astype(F32).astype(BF16)
    pick1 = (row == ids[1:2, :] * CAP + slot1).astype(F32).astype(BF16)
    pick0_ref[...] = pick0
    pick1_ref[...] = pick1
    grad = grad_ref[...].astype(F32)
    scaled0 = (gates_ref[:, 0:1] * grad).astype(BF16)
    scaled1 = (gates_ref[:, 1:2] * grad).astype(BF16)
    sent = mm(pick0, scaled0, 1, 0) + mm(pick1, scaled1, 1, 0)
    send_ref[...] = sent.astype(BF16).reshape(send_ref.shape)


def norm_kernel(tok_ref, gate_ref, pick0_ref, pick1_ref, normed_ref, send_ref):
    heads = [tok_ref[h].astype(F32) for h in range(tok_ref.shape[0])]
    width = HEAD_DIM * len(heads)
    total = heads[0]
    for h in heads[1:]:
        total = total + h
    mean = jnp.sum(total, axis=1, keepdims=True) * (1.0 / width)
    squares = None
    for h in heads:
        c = h - mean
        squares = c * c if squares is None else squares + c * c
    variance = jnp.sum(squares, axis=1, keepdims=True) * (1.0 / width)
    scale = lax.rsqrt(variance + 1e-05)
    for n, h in enumerate(heads):
        cols = slice(n * HEAD_DIM, (n + 1) * HEAD_DIM)
        normed_ref[:, cols] = ((h - mean) * scale * gate_ref[:, cols].astype(F32)).astype(BF16)
    pick = pick0_ref[...] + pick1_ref[...]
    send_ref[...] = mm(pick, normed_ref[...], 1, 0).astype(BF16).reshape(send_ref.shape)


def hidden_grad_kernel(grad_ref, down_ref, out_ref):
    grads = grad_ref[...].reshape(ROWS, grad_ref.shape[2])
    out_ref[0] = mm(grads, down_ref[0], 1, 1)


def expert_in_kernel(in_ref, hg_ref, gate_ref, up_ref, hidden_ref, gg_ref, ug_ref):
    rows = in_ref[...].reshape(ROWS, in_ref.shape[2])
    gate_pre = mm(rows, gate_ref[0], 1, 0)
    up_pre = mm(rows, up_ref[0], 1, 0)
    sigma = jax.nn.sigmoid(gate_pre)
    silu = gate_pre * sigma
    hidden_grad = hg_ref[0]
    hidden_ref[0] = (silu * up_pre).astype(BF16)
    gg_ref[0] = (hidden_grad * up_pre * (sigma * (1.0 + gate_pre * (1.0 - sigma)))).astype(BF16)
    ug_ref[0] = (hidden_grad * silu).astype(BF16)


def weight_grad(table, offset, source, act, groups, turned):
    cols = source.shape[2] // 8
    hid = act.shape[2]
    piece = (hid, cols) if turned else (cols, hid)

    def kernel(order_ref, src, act_ref, *outs):
        sides = [act_ref[e].T if turned else act_ref[e] for e in range(2)]
        for out, (first, count, experts) in zip(outs, groups):
            for n in range(count):
                owner = order_ref[offset + first + n]
                at = pl.ds(pl.multiple_of(owner * cols, cols), cols)
                for m, e in enumerate(experts):
                    rows = src[:, e * CAP : (e + 1) * CAP, at].reshape(ROWS, cols)
                    side = sides[e]
                    grad = mm(side, rows, 1, 0) if turned else mm(rows, side, 0, 0)
                    out[n, m] = grad.astype(BF16)

    return pl.pallas_call(
        kernel,
        out_shape=tuple(jax.ShapeDtypeStruct((c, len(x), *piece), BF16) for _, c, x in groups),
        in_specs=[smem(), vmem(), vmem()],
        out_specs=(vmem(),) * len(groups),
    )(table, source, act)


def relay_kernel(near1_ref, far1_ref, near3_ref, far3_ref, out1_ref, out3_ref):
    out1_ref[...] = (near1_ref[...].astype(F32) + far1_ref[...].astype(F32)).astype(BF16)
    out3_ref[...] = (near3_ref[...].astype(F32) + far3_ref[...].astype(F32)).astype(BF16)


def row_sum_kernel(own_ref, a1_ref, a3_ref, b1_ref, b3_ref, keep_ref, send_ref):
    for e, (one, three) in enumerate(((a1_ref, a3_ref), (b1_ref, b3_ref))):
        for n, out in enumerate((keep_ref, send_ref)):
            total = own_ref[n, e].astype(F32) + one[n, 0].astype(F32) + three[n, 0].astype(F32)
            out[e] = total.astype(out.dtype)


def expert_back_kernel(hidden_ref, down_ref, gg_ref, ug_ref, gate_ref, up_ref, out_ref):
    step = pl.program_id(0)
    shape = out_ref.shape

    @pl.when(step < 2)
    def _():
        out_ref[...] = mm(hidden_ref[0], down_ref[0], 1, 0).astype(BF16).reshape(shape)

    @pl.when(step >= 2)
    def _():
        total = mm(gg_ref[0], gate_ref[0], 1, 1) + mm(ug_ref[0], up_ref[0], 1, 1)
        out_ref[...] = total.astype(BF16).reshape(shape)


def pair_sum_kernel(keep_ref, got_ref, *outs):
    for n, out in enumerate(outs):
        out[...] = (keep_ref[n].astype(F32) + got_ref[n].astype(F32)).astype(out.dtype)


def mixed_kernel(back_ref, pick0_ref, pick1_ref, gates_ref, out_ref):
    back = back_ref[:, 0:2].reshape(EXPERTS * CAP, back_ref.shape[3])
    first = mm(pick0_ref[...], back, 0, 0) * gates_ref[:, 0:1]
    second = mm(pick1_ref[...], back, 0, 0) * gates_ref[:, 1:2]
    out_ref[...] = (first + second).astype(BF16)


def normed_grad_kernel(back_ref, pick0_ref, pick1_ref, out_ref):
    back = back_ref[:, 2:4].reshape(EXPERTS * CAP, back_ref.shape[3])
    pick = pick0_ref[...] + pick1_ref[...]
    out_ref[...] = mm(pick, back, 0, 0).astype(BF16)


def move_y(value, distance, keep=lambda hi, y: True):
    pairs = [
        (hi * 4 + y, hi * 4 + (y + distance) % 4)
        for hi in range(2)
        for y in range(4)
        if keep(hi, y)
    ]
    return lax.ppermute(value, "ctx", pairs)


def move_x(value, both=True):
    pairs = [(y, 4 + y) for y in range(4)]
    if both:
        pairs += [(4 + y, y) for y in range(4)]
    return lax.ppermute(value, "ctx", pairs)


def along_row(pieces):
    one_a, one_b, two_a, two_b, three_a, three_b, _ = pieces
    far1 = move_y(two_a, 1)
    far3 = move_y(two_b, 3)
    b1 = move_y(one_b, 1)
    a3 = move_y(three_a, 3)
    both1, both3 = pl.pallas_call(
        relay_kernel,
        out_shape=(
            jax.ShapeDtypeStruct(one_a.shape, BF16),
            jax.ShapeDtypeStruct(one_a.shape, BF16),
        ),
        in_specs=[vmem()] * 4,
        out_specs=(vmem(),) * 2,
        name="relay",
    )(one_a, far1, three_b, far3)
    a1 = move_y(both1, 1)
    b3 = move_y(both3, 3)
    return a1, a3, b1, b3


def exchange(value):
    return lax.all_to_all(value, "exp", split_axis=0, concat_axis=0, tiled=True)


ROW_GROUPS = tuple((n, 2, (e,)) for n in (0, 2, 4) for e in (0, 1)) + ((6, 2, (0, 1)),)
AT_NEAR, AT_FAR, AT_REST, AT_Y, AT_X = 0, 4, 6, 8, 16


def shard_table():
    lines = []
    for shard in range(8):
        hi, y = divmod(shard, 4)
        low, high = int(hi == 0), hi
        line = [2 * low, int(y >= 1), high, int(y >= 3), 2 * low, high, int(y >= 2), 0]
        for n in (1, 2, 3, 0):
            line += [hi * 4 + (y + n) % 4, (1 - hi) * 4 + (y + n) % 4]
        line += [(1 - hi) * 4 + (y + n) % 4 for n in range(4)]
        line += [hi * 4 + (y + n) % 4 for n in range(4)]
        lines.append(line)
    return np.asarray(lines, np.int32)


def step(queries, keys, values, gate_input, route_ids, route_gates, w_gate, w_up, w_down, out_grad):
    width = gate_input.shape[1]
    hid = w_gate.shape[2]
    ctx = lax.axis_index("ctx")
    full = jax.ShapeDtypeStruct
    down_x = [(n, 4 + n) for n in range(4)]
    table = lax.dynamic_index_in_dim(jnp.asarray(shard_table()), ctx, 0, keepdims=False)

    kv = jnp.stack([keys, values])
    from_y1 = move_y(kv, 1, lambda hi, y: hi == 0 or y < 3)
    from_x = move_x(jnp.where(ctx >= 4, queries[None], kv))
    from_y3 = move_y(kv, 3, lambda hi, y: y == 0)
    from_y2 = move_y(from_y1, 1, lambda hi, y: hi == 0 or y in (1, 2))
    from_xy3 = move_y(from_x, 3, lambda hi, y: hi == 1)

    pick0, pick1, send_grads = pl.pallas_call(
        route_kernel,
        out_shape=(
            full((EXPERTS * CAP, TOK), BF16),
            full((EXPERTS * CAP, TOK), BF16),
            full((N_EXP, 2 * CAP, width), BF16),
        ),
        in_specs=[vmem()] * 3,
        out_specs=(vmem(),) * 3,
        name="route",
    )(route_ids.T, route_gates, out_grad)
    recv_grads = exchange(send_grads)

    acc = attend_own(queries, kv)
    acc, lent = attend(
        table,
        AT_NEAR,
        ((1, 0), (0, 0), (0, 1), (0, 2)),
        [queries, from_x],
        [from_y1, from_x, from_y3],
        [acc, None],
        (F32, F32),
    )
    acc, lent = attend(
        table,
        AT_FAR,
        ((1, 0), (0, 1)),
        [queries, from_x],
        [from_y2, from_xy3],
        [acc, lent],
        (F32, BF16),
    )
    returned = lax.ppermute(lent, "ctx", down_x)
    (acc,) = attend(table, AT_REST, ((0, 0),), [queries], [from_y2], [acc], (F32,))
    attended = (acc + returned.astype(F32)).astype(BF16)

    expert_block = pl.BlockSpec((N_EXP, CAP, width), lambda e: (0, e, 0))
    in_weight = pl.BlockSpec((1, width, hid), lambda e: (e, 0, 0))
    out_weight = pl.BlockSpec((1, hid, width), lambda e: (e, 0, 0))
    act_block = pl.BlockSpec((1, ROWS, hid), lambda e: (e, 0, 0))
    attended, recv_grads = lax.optimization_barrier((attended, recv_grads))
    token_heads = exchange(attended.reshape(N_EXP, TOK, HEAD_DIM))
    hidden_grad = pl.pallas_call(
        hidden_grad_kernel,
        grid=(2,),
        out_shape=full((2, ROWS, hid), F32),
        in_specs=[expert_block, out_weight],
        out_specs=act_block,
        name="hg",
    )(recv_grads, w_down)
    normed, send_inputs = pl.pallas_call(
        norm_kernel,
        out_shape=(full((TOK, width), BF16), full((N_EXP, 2 * CAP, width), BF16)),
        in_specs=[vmem()] * 4,
        out_specs=(vmem(),) * 2,
        name="norm",
    )(token_heads, gate_input, pick0, pick1)
    recv_inputs = exchange(send_inputs)

    act = full((2, ROWS, hid), BF16)
    hidden, gate_grad, up_grad = pl.pallas_call(
        expert_in_kernel,
        grid=(2,),
        out_shape=(act, act, act),
        in_specs=[expert_block, act_block, in_weight, in_weight],
        out_specs=(act_block,) * 3,
        name="expert_in",
    )(recv_inputs, hidden_grad, w_gate, w_up)

    ga = weight_grad(table, AT_Y, recv_inputs, gate_grad, ROW_GROUPS, False)
    got_g = along_row(ga)
    up_send, up_keep, *ua = weight_grad(
        table,
        0,
        recv_inputs,
        up_grad,
        ((AT_X, 4, (0,)), (AT_X + 4, 4, (0,))) + tuple((AT_Y + n, 2, (1,)) for n in (0, 2, 4, 6)),
        False,
    )
    up_got = move_x(up_send)
    do = weight_grad(table, AT_Y, recv_grads, hidden, ROW_GROUPS, True)
    got_d = along_row(do)
    got_a = []
    for n in range(3):
        got_a.append(move_y(ua[n], n + 1))
    early = lambda shape: pl.BlockSpec((1, *shape), lambda n: (jnp.minimum(n, 1), 0, 0))
    late = lambda shape: pl.BlockSpec((1, *shape), lambda n: (jnp.maximum(n - 2, 0), 0, 0))
    expert_back = pl.pallas_call(
        expert_back_kernel,
        grid=(4,),
        out_shape=full((N_EXP, 4, CAP, width), BF16),
        in_specs=[
            early((ROWS, hid)),
            early((hid, width)),
            late((ROWS, hid)),
            late((ROWS, hid)),
            late((width, hid)),
            late((width, hid)),
        ],
        out_specs=pl.BlockSpec((N_EXP, 1, CAP, width), lambda n: (0, n, 0, 0)),
        name="expert_back",
    )(hidden, w_down, gate_grad, up_grad, w_gate, w_up)
    back = exchange(expert_back)

    token = full((TOK, width), BF16)
    mixed = pl.pallas_call(
        mixed_kernel, out_shape=token, in_specs=[vmem()] * 4, out_specs=vmem(), name="mixed"
    )(back, pick0, pick1, route_gates)
    normed_grad = pl.pallas_call(
        normed_grad_kernel, out_shape=token, in_specs=[vmem()] * 3, out_specs=vmem(), name="ngrad"
    )(back, pick0, pick1)

    wide = lambda v: v.astype(F32)

    def over_row(own, got):
        shape = own.shape[1:]
        return pl.pallas_call(
            row_sum_kernel,
            out_shape=(full(shape, F32), full(shape, BF16)),
            in_specs=[vmem()] * 5,
            out_specs=(vmem(),) * 2,
            name="row_sum",
        )(own, *got)

    gate_part, gate_send = over_row(ga[6], got_g)
    gate_got = move_x(gate_send)
    sums = wide(ua[3]) + wide(got_a[0]) + wide(got_a[1]) + wide(got_a[2])
    up_sent = sums[1].astype(BF16)
    got_ax = move_x(up_sent)
    quarter = up_keep.shape[1:]
    up_part, *up_rest = pl.pallas_call(
        pair_sum_kernel,
        out_shape=(full(quarter, F32),) + (full(quarter, BF16),) * 3,
        in_specs=[vmem()] * 2,
        out_specs=(vmem(),) * 4,
        name="pair_sum",
    )(up_keep, up_got)
    got_u = []
    for n in (1, 2, 3):
        got_u.append(move_y(up_rest[n - 1], n))
    _, gate_got, *got_u = lax.optimization_barrier((up_sent, gate_got, *got_u))
    gate_sum = (gate_part + wide(gate_got)).astype(BF16)
    up_first = (up_part + wide(got_u[0]) + wide(got_u[1]) + wide(got_u[2])).astype(BF16)
    up_last = (sums[0] + wide(got_ax)).astype(BF16)
    up_sum = jnp.concatenate([up_first, up_last])
    down_part, down_send = over_row(do[6], got_d)
    down_got = move_x(down_send)
    down_sum = (down_part + wide(down_got)).astype(BF16)
    return (normed, mixed, normed_grad, gate_sum, up_sum, down_sum)


def solution(mesh):
    in_specs = (
        P("ctx", "exp"),
        P("ctx", "exp"),
        P("ctx", "exp"),
        P(("ctx", "exp"), None),
        P(("ctx", "exp"), None),
        P(("ctx", "exp"), None),
        P("exp", None, None),
        P("exp", None, None),
        P("exp", None, None),
        P(("ctx", "exp"), None),
    )
    out_specs = (
        P(("ctx", "exp"), None),
        P(("ctx", "exp"), None),
        P(("ctx", "exp"), None),
        P("exp", "ctx", None),
        P("exp", "ctx", None),
        P("exp", None, "ctx"),
    )
    return jax.shard_map(step, mesh=mesh, in_specs=in_specs, out_specs=out_specs, check_vma=False)
```
